128 devices in a mesh: row: 8 (over x, core), col: 16 (over y, z).
Axes of the slice: x: 4, y: 4, z: 4, core: 2. Of those that a mesh axis runs over, the one named last changes fastest.
Arguments:
- start_columns: bfloat16 [32768, 8192], P('row', 'col'), may hold values from -6 to 6
- hamiltonian: bfloat16 [128, 2, 256, 256], P(('row', 'col')), may hold values from -0.09375 to 0.09375
- band_pattern: int32 [128], P(('row', 'col')), may hold values 0 or 1
- coefficients: float32 [4], replicated, may hold values from -1 to 1
- tile_peer: int32 [2048, 1], P(('row', 'col')), may hold values from 0 to 15; in each aligned block of 16 rows (0 to 15, 16 to 31, ...) at most 2 rows name the same one
- tile_block: int32 [2048], P(('row', 'col')), may hold values from 0 to 7
- tile_count: int32 [512], P(('row', 'col')), may hold values from 1 to 4
- basis_values: bfloat16 [2048, 2, 512, 128], P(('row', 'col')), may hold values from -6 to 6
- core_density: float32 [512, 128], P(('row', 'col')), may hold values from 0.5 to 3
Outputs:
- density: float32 [512, 128], P(('row', 'col'))
- h_update: bfloat16 [32768, 8192], P('row', 'col')
The draws below stay inside these ranges and needn't reach their ends.
Inputs may be any that keep to these rules, and one draw needn't show every extreme that they name: `tile_peer`: the entries of one device name one col index at most 2 times, and on some device exactly 2 times.
All inputs are finite; a program needn't handle non-finite values. No bound on the sum of `band_pattern` on one device may be relied on, other than what follows from the above.
Results may differ from the reference program's by a relative error of at most 0.0059.
Values may be sent and summed in bfloat16 or wider, within the bound.
A program may use at most 192 MiB of HBM per device.

```python
import math
import jax
import jax.numpy as jnp
import numpy as np
from jax import lax

W = 256
KB = 512
DEG = 3
TILES_DEV = 4
SLOTS = 4
CAP = 2
P_SIZE = 128
FUNCS = 32768
COLS = 8192
KROW = 8
NBLK = 128
TILES = 512
ENTRIES = 2048
N_COL = 16


def set_ends(array, key, low, largest):
    spot = [jax.random.randint(jax.random.fold_in(key, axis), (), 0, length) for axis, length in enumerate(array.shape)]
    longest = array.shape.index(max(array.shape))
    beside = spot[:longest] + [(spot[longest] + 1) % array.shape[longest]] + spot[longest + 1:]
    return array.at[tuple(spot)].set(low).at[tuple(beside)].set(largest)


def block_levels(key, extent, split, smallest, top_value):
    factor_of = 1.0
    for position, parts in split:
        steps = jax.random.uniform(jax.random.fold_in(jax.random.fold_in(key, 6), position), (parts,), jnp.float32, smallest / len(split), top_value / len(split))
        factor_of = factor_of * jnp.repeat(jnp.exp(steps), extent[position] // parts).reshape((-1,) + (1,) * (len(extent) - 1 - position))
    return factor_of


def assign_block(key, own, number, rows, count, top, limit, lean):
    order = jax.random.permutation(key, count)
    heavy_load, common = shares(count, rows * top, limit, lean, True), shares(count, rows * top, limit, lean, False)
    places = jnp.arange(count)

    def named(sizes, offset_by):
        used = int((sizes > 0).sum())
        fixed = max(1, used // 4)
        moved = fixed + (places - fixed + offset_by * (used - fixed)) % max(1, count - fixed)
        return jnp.zeros((count,), jnp.int32).at[order[jnp.where(places < fixed, places, moved)]].set(jnp.asarray(sizes, jnp.int32))

    sizes = jnp.where(number % 4 == 0, named(heavy_load, number // 4), named(common, number - number // 4 - 1))
    mixed = jax.random.permutation(jax.random.fold_in(own, 3), count)
    source_of, sink = mixed[0:count // 2 * 2:2], mixed[1:count // 2 * 2:2]
    room = jnp.minimum(sizes[source_of] - 1, limit - sizes[sink]) // 2
    room = jnp.where((source_of == order[0]) | (sink == order[0]) | (sizes[sink] == 0), 0, jnp.maximum(room, 0))
    moved = jax.random.randint(jax.random.fold_in(own, 4), (count // 2,), 0, 1 << 20) % (room + 1)
    sizes = sizes.at[source_of].add(-moved).at[sink].add(moved)
    items = jnp.searchsorted(jnp.cumsum(sizes), jnp.arange(rows * top), side="right").astype(jnp.int32)
    table = items.reshape(top, rows).T
    table = table[jax.random.permutation(jax.random.fold_in(own, 1), rows)]
    offset_by = jax.random.randint(jax.random.fold_in(own, 2), (rows, 1), 0, top)
    return jnp.take_along_axis(table, (jnp.arange(top)[None, :] + offset_by) % top, axis=1)


def shares(number_of, total, reach, slope, full):
    weights = [(1 << 20) // math.isqrt(rank ** slope) + 1 for rank in range(1, number_of + 1)]
    largest = reach if full else min(reach, max(-(-total // number_of), total * weights[0] // sum(weights)))
    least = 1 if total - largest >= number_of - 1 else 0
    holding, surplus = [largest] + [least] * (number_of - 1), total - largest - least * (number_of - 1)
    while surplus > 0:
        candidates = [i for i in range(1, number_of) if holding[i] < largest] or [i for i in range(1, number_of) if holding[i] < reach]
        mass, left = sum([weights[i] for i in candidates]), surplus
        for i in candidates:
            extra = min(reach - holding[i], max(1, left * weights[i] // mass), surplus)
            holding[i] = holding[i] + extra
            surplus = surplus - extra
    return np.array(holding)


def centred(rng, extent, scale, bound, shards=(), kind=jnp.bfloat16):
    level = block_levels(rng, extent, shards, -0.22, 0.18) if shards else 1.0
    drawn = jax.random.normal(rng, extent, jnp.float32) * scale * level
    return jnp.minimum(jnp.maximum(drawn, -bound), bound).astype(kind)


def setup_inputs(seed: int = 0) -> dict:
    seeds = jax.random.split(jax.random.key(seed), 10)
    start_columns = centred(seeds[0], (FUNCS, COLS), 1.0, 6.0, ((0, 8), (1, 16)))
    hamiltonian = centred(seeds[1], (NBLK, 2, W, W), (16 * W) ** -0.5, 0.09375, ((0, 128),))
    band_pattern = set_ends((jax.random.randint(seeds[2], (NBLK,), 0, 4) < 3).astype(jnp.int32), jax.random.fold_in(seeds[2], 1), 0, 1)
    coefficients = jnp.clip(jax.random.uniform(seeds[3], (DEG + 1,), jnp.float32, -1.0, 1.0), -1.0, 1.0)
    tile_peer_keys = jax.random.split(jax.random.fold_in(seeds[4], 1), ENTRIES // (TILES_DEV * SLOTS))
    tile_peer_turns = jax.random.permutation(jax.random.fold_in(seeds[4], 3), ENTRIES // (TILES_DEV * SLOTS))
    tile_peer = jax.vmap(lambda own, number: assign_block(jax.random.fold_in(seeds[4], 2), own, number, TILES_DEV * SLOTS, N_COL, 1, CAP, 2))(tile_peer_keys, tile_peer_turns).reshape((ENTRIES, 1))
    tile_block = set_ends(jax.random.randint(seeds[5], (ENTRIES,), 0, KROW), jax.random.fold_in(seeds[5], 1), 0, KROW - 1).astype(jnp.int32)
    tile_count = set_ends(jax.random.randint(seeds[6], (TILES,), 1, SLOTS + 1), jax.random.fold_in(seeds[6], 1), 1, SLOTS).astype(jnp.int32)
    basis_values = centred(seeds[7], (ENTRIES, 2, KB, P_SIZE), 1.0, 6.0, ((0, 128),))
    core_density = jnp.clip(jnp.exp(math.log(3.0) - 1.7917595 * jax.random.uniform(seeds[8], (TILES, P_SIZE), jnp.float32) ** block_levels(seeds[8], (TILES, P_SIZE), ((0, 128),), -0.2, 0.2)), 0.5, 3.0)
    return {"start_columns": start_columns, "hamiltonian": hamiltonian, "band_pattern": band_pattern, "coefficients": coefficients, "tile_peer": tile_peer, "tile_block": tile_block, "tile_count": tile_count, "basis_values": basis_values, "core_density": core_density}


exchange_factor = (3.0 / math.pi) ** (1.0 / 3.0)

def band_apply(columns, diagonal_blocks, lower_band, upper_band):
    split_rows = columns.astype(jnp.float32).reshape(NBLK, W, columns.shape[1])
    zero_block = jnp.zeros_like(split_rows[:1])
    previous = jnp.concatenate([zero_block, split_rows[:-1]], axis=0)
    following = jnp.concatenate([split_rows[1:], zero_block], axis=0)
    product = jnp.einsum('nij,njc->nic', diagonal_blocks, split_rows)
    product = product + jnp.einsum('nij,njc->nic', lower_band, previous)
    product = product + jnp.einsum('nij,njc->nic', upper_band, following)
    return product.reshape(FUNCS, columns.shape[1])

def reference(start_columns, hamiltonian, band_pattern, coefficients, tile_peer, tile_block, tile_count, basis_values, core_density):
    band_values = hamiltonian.astype(jnp.float32)
    pattern = band_pattern.astype(jnp.float32)[:, None, None]
    diagonal_blocks = band_values[:, 0]
    coupling = band_values[:, 1]
    lower_band = jnp.triu(coupling) * pattern
    upper_band = jnp.tril(coupling, -1) * pattern

    def expand(columns):
        previous = columns.astype(jnp.float32)
        current = band_apply(columns, diagonal_blocks, lower_band, upper_band)
        kernel_sum = coefficients[0] * previous + coefficients[1] * current
        for degree in range(1, DEG):
            following = 2.0 * band_apply(current.astype(jnp.bfloat16), diagonal_blocks, lower_band, upper_band) - previous
            kernel_sum = kernel_sum + coefficients[degree + 1] * following
            previous, current = (current, following)
        return kernel_sum.astype(jnp.bfloat16)
    col_blocks = start_columns.reshape(FUNCS, N_COL, KB).transpose(1, 0, 2)
    kernel = lax.map(expand, col_blocks).transpose(1, 0, 2).reshape(FUNCS, COLS)
    entry_count = TILES_DEV * SLOTS
    entry_ids = jnp.arange(ENTRIES, dtype=jnp.int32)
    quadrature = 1.0 / math.sqrt(P_SIZE)

    def locate(entry):
        device = entry // entry_count
        row_index = device // N_COL
        row_start = ((row_index * KROW + tile_block[entry]) * KB).astype(jnp.int32)
        col_start = (tile_peer[entry, 0] * KB).astype(jnp.int32)
        is_live = (entry % SLOTS < tile_count[entry // SLOTS]).astype(jnp.float32)
        return (row_start, col_start, is_live)

    def contribute(entry):
        row_start, col_start, is_live = locate(entry)
        kernel_block = lax.dynamic_slice(kernel, (row_start, col_start), (KB, KB))
        basis_pair = basis_values[entry]
        projected = jnp.dot(kernel_block.T, basis_pair[0], preferred_element_type=jnp.float32)
        return lax.optimization_barrier(jnp.sum(projected * basis_pair[1].astype(jnp.float32), axis=0)) / KB * is_live
    contrib = lax.map(contribute, entry_ids)
    density = core_density + contrib.reshape(TILES, SLOTS, P_SIZE).sum(axis=1)
    potential = -exchange_factor * jnp.cbrt(jnp.maximum(density, 0.1))

    def accumulate(total, entry):
        row_start, col_start, is_live = locate(entry)
        basis_pair = basis_values[entry]
        weighted = (basis_pair[1].astype(jnp.float32) * potential[entry // SLOTS][None, :]).astype(jnp.bfloat16)
        update_block = jnp.dot(basis_pair[0], weighted.T, preferred_element_type=jnp.float32) * quadrature
        update_block = (update_block * is_live).astype(jnp.bfloat16).astype(jnp.float32)
        previous_sum = lax.dynamic_slice(total, (row_start, col_start), (KB, KB))
        total = lax.dynamic_update_slice(total, previous_sum + update_block, (row_start, col_start))
        return (total, None)
    total = lax.scan(accumulate, jnp.zeros((FUNCS, COLS), jnp.float32), entry_ids)[0]
    return (density, total.astype(jnp.bfloat16))
```

```python
import functools
import math

import jax
import jax.numpy as jnp
from jax import lax
from jax.experimental import pallas as pl
from jax.experimental.pallas import tpu as pltpu
from jax.sharding import PartitionSpec as P

MESH = pl.DeviceIdType.MESH
W = 256
KB = 512
SLOTS = 4
CAP = 2
P_SIZE = 128
NB = 16
ENTRIES = 16
PIECES = 4
SIDE = 4
OFFSETS = tuple((k // SIDE, k % SIDE) for k in range(1, NB))

exchange_factor = (3.0 / math.pi) ** (1.0 / 3.0)


def exchange_kernel(
    columns,
    ham,
    pattern,
    coef,
    peers,
    tile_block,
    tile_count,
    basis,
    core,
    dens,
    received,
    pot_in,
    block_of,
    own_ham,
    bands,
    band,
    v0,
    v1,
    v2,
    total,
    kern,
    basis_vm,
    outgoing,
    incoming,
    meta_out,
    meta_in,
    meta_sm,
    contrib_out,
    contrib_in,
    pot_out,
    pot_got,
    owner,
    request,
    local_sem,
    out_sem,
    band_send,
    band_recv,
    meta_send,
    meta_recv,
    halo_send,
    halo_recv,
    basis_send,
    basis_recv,
    contrib_send,
    contrib_recv,
    pot_send,
    pot_recv,
):
    r = lax.axis_index("row")
    c = lax.axis_index("col")
    rows = lax.axis_size("row")
    y, z = c // SIDE, c % SIDE
    rows_here = NB * W

    def at(dy, dz):
        return lax.rem(y + dy + SIDE, SIDE) * SIDE + lax.rem(z + dz + SIDE, SIDE)

    def remote(src, dst, send, recv, **where):
        return pltpu.make_async_remote_copy(
            src_ref=src, dst_ref=dst, send_sem=send, recv_sem=recv, device_id=where, device_id_type=MESH
        )

    up, down = lax.rem(r + 1, rows), lax.rem(r + rows - 1, rows)

    barrier = pltpu.get_barrier_semaphore()
    for dy, dz in OFFSETS:
        pl.semaphore_signal(barrier, inc=1, device_id={"col": at(dy, dz)}, device_id_type=MESH)
    for row in (up, down):
        pl.semaphore_signal(barrier, inc=1, device_id={"row": row}, device_id_type=MESH)

    load_diag = pltpu.make_async_copy(ham.at[0, 0], bands.at[0, c], local_sem.at[0])
    load_coupling = pltpu.make_async_copy(ham.at[0, 1], own_ham, local_sem.at[1])
    load_basis = pltpu.make_async_copy(basis, basis_vm, local_sem.at[2])
    load_columns = pltpu.make_async_copy(columns, v0.at[pl.ds(W, rows_here)], local_sem.at[3])
    load_diag.start()
    load_coupling.start()
    load_basis.start()
    load_columns.start()

    row_id = lax.broadcasted_iota(jnp.int32, (8, P_SIZE), 0)
    for k in range(NB):
        peer = at(k // SIDE, k % SIDE)
        first, second = jnp.int32(ENTRIES), jnp.int32(ENTRIES)
        for e in reversed(range(ENTRIES)):
            named = peers[e, 0] == peer
            second = jnp.where(named, first, second)
            first = jnp.where(named, jnp.int32(e), first)
        wanted = []
        for s, found in enumerate((first, second)):
            entry = jnp.minimum(found, ENTRIES - 1)
            live = (found < ENTRIES) & (lax.rem(entry, SLOTS) < tile_count[lax.div(entry, SLOTS)])
            wanted.append(jnp.where(live, tile_block[entry], -1))
            owner[s * NB + k] = entry
            request[s * NB + k] = wanted[s]
        words = jnp.where(row_id == 0, wanted[0], wanted[1])
        if k == 0:
            meta_in[0] = words
        else:
            meta_out[k] = words

    load_coupling.wait()
    bands[1, c] = (own_ham[...].astype(jnp.float32) * pattern[0].astype(jnp.float32)).astype(jnp.bfloat16)
    load_diag.wait()
    pl.semaphore_wait(barrier, NB - 1 + 2)

    def band_copy(half, dy, dz):
        if half == 0:
            source, there = at(0, -dz), (at(dy, 0) if dy else at(0, dz))
            source = source if dy else c
        else:
            source, there = at(-dy, 0), (at(0, dz) if dz else at(dy, 0))
            source = source if dz else c
        i = half * (NB - 1) + dy * SIDE + dz - 1
        return remote(bands.at[half, source], bands.at[half, source], band_send.at[i], band_recv.at[i], col=there)

    def band_wait(half, dy, dz):
        i = half * (NB - 1) + dy * SIDE + dz - 1
        block = bands.at[half, at(-dy, -dz)]
        remote(block, block, band_send.at[i], band_recv.at[i], col=at(dy, dz)).wait_recv()

    for d in range(1, SIDE):
        band_copy(0, 0, d).start()
        band_copy(1, d, 0).start()
    halo_up = [remote(columns.at[pl.ds(rows_here - W, W)], v0.at[pl.ds(0, W)], halo_send.at[0], halo_recv.at[0], row=up)]
    halo_down = [remote(columns.at[pl.ds(0, W)], v0.at[pl.ds(rows_here + W, W)], halo_send.at[1], halo_recv.at[1], row=down)]
    for degree, v in ((1, v1), (2, v2)):
        halo_up.append(
            remote(v.at[pl.ds(rows_here, W)], v.at[pl.ds(0, W)], halo_send.at[2 * degree], halo_recv.at[2 * degree], row=up)
        )
        halo_down.append(
            remote(
                v.at[pl.ds(W, W)],
                v.at[pl.ds(rows_here + W, W)],
                halo_send.at[2 * degree + 1],
                halo_recv.at[2 * degree + 1],
                row=down,
            )
        )
    halo_up[0].start()
    halo_down[0].start()
    meta_copies = [
        remote(meta_out.at[k], meta_in.at[k], meta_send.at[k], meta_recv.at[k], col=at(k // SIDE, k % SIDE))
        for k in range(1, NB)
    ]
    for copy in meta_copies:
        copy.start()

    load_basis.wait()
    for s in range(CAP):
        incoming[s * NB] = basis_vm[owner[s * NB]]

        def pack(k, carry, s=s):
            outgoing[s * NB + k] = basis_vm[owner[s * NB + k]]
            return carry

        lax.fori_loop(1, NB, pack, 0)

    for d in range(SIDE):
        if d:
            band_wait(0, 0, d)
            band_wait(1, d, 0)
        for other in range(1, SIDE):
            band_copy(0, other, d).start()
            band_copy(1, d, other).start()

    pieces = [(half, first) for half in range(2) for first in range(0, KB, 2 * KB // PIECES)]
    part = 2 * KB // PIECES
    for s in range(CAP):
        for half, first in pieces:
            for dy, dz in OFFSETS:
                i = s * NB + dy * SIDE + dz
                remote(
                    outgoing.at[i, half, pl.ds(first, part)],
                    incoming.at[i, half, pl.ds(first, part)],
                    basis_send.at[i],
                    basis_recv.at[i],
                    col=at(dy, dz),
                ).start()

    for half in range(2):
        for dy, dz in OFFSETS:
            if (half == 0 and dy) or (half == 1 and dz):
                band_wait(half, dy, dz)

    row_at = lax.broadcasted_iota(jnp.int32, (W, W), 0)
    col_at = lax.broadcasted_iota(jnp.int32, (W, W), 1)

    def build(j, carry):
        coupling = bands[1, j].astype(jnp.float32)
        first = jnp.where((j == 0) & (r == 0), 0.0, 1.0)
        last = jnp.where((j == NB - 1) & (r == rows - 1), 0.0, 1.0)
        band[j, :, 0:W] = (jnp.where(col_at >= row_at, coupling, 0.0) * first).astype(jnp.bfloat16)
        band[j, :, W : 2 * W] = bands[0, j]
        band[j, :, 2 * W : 3 * W] = (jnp.where(col_at < row_at, coupling, 0.0) * last).astype(jnp.bfloat16)
        return carry

    lax.fori_loop(0, NB, build, 0)

    def apply(j, v):
        window = v[pl.ds(pl.multiple_of(j * W, W), 3 * W), :]
        return jnp.dot(band[j], window, preferred_element_type=jnp.float32)

    def inner(j):
        return pl.ds(pl.multiple_of((j + 1) * W, W), W)

    def degree_1(j, carry):
        value = apply(j, v0)
        total[j] = value
        v1[inner(j), :] = value.astype(jnp.bfloat16)
        return carry

    c0, c1, c2, c3 = (coef[i] for i in range(4))

    def degree_2(j, carry):
        start = v0[inner(j), :].astype(jnp.float32)
        value = 2.0 * apply(j, v1) - start
        v2[inner(j), :] = value.astype(jnp.bfloat16)
        total[j] = c0 * start + (c1 - c3) * total[j] + c2 * value
        return carry

    def degree_3(j, carry):
        value = total[j] + (2.0 * c3) * apply(j, v2)
        kern[j // 2, pl.ds(pl.multiple_of(lax.rem(j, 2) * W, W), W), :] = value.astype(jnp.bfloat16)
        return carry

    load_columns.wait()
    halo_up[0].wait()
    halo_down[0].wait()
    for step, degree in ((degree_1, 1), (degree_2, 2)):
        step(0, 0)
        step(NB - 1, 0)
        lax.fori_loop(1, NB // 2, step, 0)
        halo_up[degree].start()
        halo_down[degree].start()
        lax.fori_loop(NB // 2, NB - 1, step, 0)
        halo_up[degree].wait()
        halo_down[degree].wait()
    lax.fori_loop(0, NB, degree_3, 0)

    for copy in meta_copies:
        copy.wait()
    meta_copy = pltpu.make_async_copy(meta_in, meta_sm, local_sem.at[4])
    meta_copy.start()
    meta_copy.wait()
    for s in range(CAP):
        for k in range(NB):
            block_of[s * NB + k] = meta_sm[k, s, 0]

    def basis_copy(i):
        return remote(outgoing.at[i], incoming.at[i], basis_send.at[i], basis_recv.at[i], col=at(0, 1))

    def project(s, k):
        i = s * NB + k
        keep = pltpu.make_async_copy(incoming.at[i], received.at[i], out_sem.at[i])
        keep.start()
        block = jnp.maximum(meta_sm[k, s, 0], 0)
        product = jnp.dot(kern[block], incoming[i, 1], preferred_element_type=jnp.float32)
        return jnp.sum(product * incoming[i, 0].astype(jnp.float32), axis=0, keepdims=True) * (1.0 / KB)

    for s in range(CAP):
        contrib_in[0, s : s + 1, :] = project(s, 0)

        def step(k, carry, s=s):
            basis_copy(s * NB + k).wait_recv()
            contrib_out[k, s : s + 1, :] = project(s, k)
            return carry

        lax.fori_loop(1, NB, step, 0)

    contrib_copies = [
        remote(
            contrib_out.at[k],
            contrib_in.at[k],
            contrib_send.at[k],
            contrib_recv.at[k],
            col=at(-(k // SIDE), -(k % SIDE)),
        )
        for k in range(1, NB)
    ]
    for copy in contrib_copies:
        copy.start()
    for copy in contrib_copies:
        copy.wait()

    potentials = []
    for t in range(ENTRIES // SLOTS):
        density = core[t : t + 1, :]
        for slot in range(SLOTS):
            e = t * SLOTS + slot
            there = peers[e, 0]
            k = lax.rem(lax.div(there, SIDE) + SIDE - y, SIDE) * SIDE + lax.rem(lax.rem(there, SIDE) + SIDE - z, SIDE)
            both = contrib_in[k]
            mine = jnp.where(owner[k] == e, both[0:1], both[1:2])
            density = density + jnp.where(slot < tile_count[t], mine, 0.0)
        dens[t : t + 1, :] = density
        x = jnp.maximum(density, 0.1)
        root = jnp.exp(jnp.log(x) * (1.0 / 3.0))
        root = root - (root * root * root - x) / (3.0 * root * root)
        potentials.append(-exchange_factor * root)

    for k in range(NB):
        lines = []
        for s in range(CAP):
            tile = lax.div(owner[s * NB + k], SLOTS)
            line = potentials[0]
            for t in range(1, ENTRIES // SLOTS):
                line = jnp.where(tile == t, potentials[t], line)
            lines.append(jnp.where(request[s * NB + k] >= 0, line, 0.0))
        words = jnp.where(row_id == 0, lines[0], lines[1])
        if k == 0:
            pot_got[0] = words
        else:
            pot_out[k] = words
    pot_copies = [
        remote(pot_out.at[k], pot_got.at[k], pot_send.at[k], pot_recv.at[k], col=at(k // SIDE, k % SIDE))
        for k in range(1, NB)
    ]
    for copy in pot_copies:
        copy.start()
    for half in range(2):
        for dy, dz in OFFSETS:
            band_copy(half, dy, dz).wait_send()

    def finish(k, carry):
        for s in range(CAP):
            basis_copy(s * NB + k).wait_send()
        return carry

    lax.fori_loop(1, NB, finish, 0)

    def kept(i, carry):
        pltpu.make_async_copy(incoming.at[i], received.at[i], out_sem.at[i]).wait()
        return carry

    lax.fori_loop(0, CAP * NB, kept, 0)
    for copy in pot_copies:
        copy.wait()
    pot_in[...] = pot_got[...]


def exchange(columns, ham, pattern, coef, peers, tile_block, tile_count, basis, core):
    any_spec = pl.BlockSpec(memory_space=pl.ANY)
    smem = pl.BlockSpec(memory_space=pltpu.SMEM)
    vmem = pl.BlockSpec(memory_space=pltpu.VMEM)
    rows_here = NB * W
    slots = CAP * NB
    bf16, f32, i32 = jnp.bfloat16, jnp.float32, jnp.int32
    dma = pltpu.SemaphoreType.DMA
    return pl.pallas_call(
        exchange_kernel,
        out_shape=(
            jax.ShapeDtypeStruct(core.shape, f32),
            jax.ShapeDtypeStruct((slots, 2, KB, P_SIZE), bf16),
            jax.ShapeDtypeStruct((NB, 8, P_SIZE), f32),
            jax.ShapeDtypeStruct((slots,), i32),
        ),
        in_specs=[any_spec, any_spec, smem, smem, smem, smem, smem, any_spec, vmem],
        out_specs=(vmem, any_spec, vmem, smem),
        scratch_shapes=[
            pltpu.VMEM((W, W), bf16),
            pltpu.VMEM((2, NB, W, W), bf16),
            pltpu.VMEM((NB, W, 3 * W), bf16),
            pltpu.VMEM((rows_here + 2 * W, KB), bf16),
            pltpu.VMEM((rows_here + 2 * W, KB), bf16),
            pltpu.VMEM((rows_here + 2 * W, KB), bf16),
            pltpu.VMEM((NB, W, KB), f32),
            pltpu.VMEM((rows_here // KB, KB, KB), bf16),
            pltpu.VMEM(basis.shape, bf16),
            pltpu.VMEM((slots, 2, KB, P_SIZE), bf16),
            pltpu.VMEM((slots, 2, KB, P_SIZE), bf16),
            pltpu.VMEM((NB, 8, P_SIZE), i32),
            pltpu.VMEM((NB, 8, P_SIZE), i32),
            pltpu.SMEM((NB, 8, P_SIZE), i32),
            pltpu.VMEM((NB, 8, P_SIZE), f32),
            pltpu.VMEM((NB, 8, P_SIZE), f32),
            pltpu.VMEM((NB, 8, P_SIZE), f32),
            pltpu.VMEM((NB, 8, P_SIZE), f32),
            pltpu.SMEM((slots,), i32),
            pltpu.SMEM((slots,), i32),
            dma((5,)),
            dma((slots,)),
            dma((2 * (NB - 1),)),
            dma((2 * (NB - 1),)),
            dma((NB,)),
            dma((NB,)),
            dma((6,)),
            dma((6,)),
            dma((slots,)),
            dma((slots,)),
            dma((NB,)),
            dma((NB,)),
            dma((NB,)),
            dma((NB,)),
        ],
        compiler_params=pltpu.CompilerParams(
            collective_id=0, has_side_effects=True, vmem_limit_bytes=66_000_000
        ),
        name="exchange",
    )(columns, ham, pattern, coef, peers, tile_block, tile_count, basis, core)


def update_kernel(block_of, pair, pot, out, total):
    i = pl.program_id(0)

    @pl.when(i == 0)
    def _():
        total[...] = jnp.zeros_like(total)

    block = block_of[i]

    @pl.when(block >= 0)
    def _():
        line = jnp.where(i < NB, pot[0, 0:1, :], pot[0, 1:2, :])
        weighted = (pair[0, 1].astype(jnp.float32) * line).astype(jnp.bfloat16)
        product = lax.dot_general(
            pair[0, 0], weighted, (((1,), (1,)), ((), ())), preferred_element_type=jnp.float32
        )
        product = (product * (1.0 / math.sqrt(P_SIZE))).astype(jnp.bfloat16).astype(jnp.float32)
        total[block] = total[block] + product

    @pl.when(i == pl.num_programs(0) - 1)
    def _():
        out[...] = total[...].astype(jnp.bfloat16)


def update(block_of, received, pot_in):
    blocks = NB * W // KB
    return pl.pallas_call(
        update_kernel,
        out_shape=jax.ShapeDtypeStruct((blocks, KB, KB), jnp.bfloat16),
        grid_spec=pltpu.PrefetchScalarGridSpec(
            num_scalar_prefetch=1,
            grid=(CAP * NB,),
            in_specs=[
                pl.BlockSpec((1, 2, KB, P_SIZE), lambda i, b: (i, 0, 0, 0)),
                pl.BlockSpec((1, 8, P_SIZE), lambda i, b: (lax.rem(i, NB), 0, 0)),
            ],
            out_specs=pl.BlockSpec((blocks, KB, KB), lambda i, b: (0, 0, 0)),
            scratch_shapes=[pltpu.VMEM((blocks, KB, KB), jnp.float32)],
        ),
        compiler_params=pltpu.CompilerParams(vmem_limit_bytes=40_000_000),
        name="update",
    )(block_of, received, pot_in)


def shards(columns, ham, pattern, coef, peers, tile_block, tile_count, basis, core):
    dens, received, pot_in, block_of = exchange(
        columns, ham, pattern, coef, peers, tile_block, tile_count, basis, core
    )
    blocks = update(block_of, received, pot_in)
    return dens, blocks.reshape(columns.shape)


def solution(mesh):
    return jax.shard_map(
        shards,
        mesh=mesh,
        in_specs=(
            P("row", "col"),
            P(("row", "col"), None, None, None),
            P(("row", "col")),
            P(),
            P(("row", "col"), None),
            P(("row", "col")),
            P(("row", "col")),
            P(("row", "col"), None, None, None),
            P(("row", "col"), None),
        ),
        out_specs=(P(("row", "col"), None), P("row", "col")),
        check_vma=False,
    )
```

```python
import functools
import math

import jax
import jax.numpy as jnp
from jax import lax
from jax.experimental import pallas as pl
from jax.experimental.pallas import tpu as pltpu
from jax.sharding import PartitionSpec as P

MESH = pl.DeviceIdType.MESH
W = 256
KB = 512
SLOTS = 4
CAP = 2
P_SIZE = 128
NB = 16
ENTRIES = 16
PIECES = 4
SIDE = 4
OFFSETS = tuple((k // SIDE, k % SIDE) for k in range(1, NB))

exchange_factor = (3.0 / math.pi) ** (1.0 / 3.0)


def exchange_kernel(
    columns,
    ham,
    pattern,
    coef,
    peers,
    tile_block,
    tile_count,
    basis,
    core,
    dens,
    received,
    pot_in,
    block_of,
    own_ham,
    bands,
    band,
    v0,
    v1,
    v2,
    total,
    kern,
    basis_vm,
    outgoing,
    incoming,
    meta_out,
    meta_in,
    meta_sm,
    contrib_out,
    contrib_in,
    pot_out,
    pot_got,
    owner,
    request,
    local_sem,
    out_sem,
    band_send,
    band_recv,
    meta_send,
    meta_recv,
    halo_send,
    halo_recv,
    basis_send,
    basis_recv,
    contrib_send,
    contrib_recv,
    pot_send,
    pot_recv,
):
    r = lax.axis_index("row")
    c = lax.axis_index("col")
    rows = lax.axis_size("row")
    y, z = c // SIDE, c % SIDE
    rows_here = NB * W

    def at(dy, dz):
        return lax.rem(y + dy + SIDE, SIDE) * SIDE + lax.rem(z + dz + SIDE, SIDE)

    def remote(src, dst, send, recv, **where):
        return pltpu.make_async_remote_copy(
            src_ref=src, dst_ref=dst, send_sem=send, recv_sem=recv, device_id=where, device_id_type=MESH
        )

    up, down = lax.rem(r + 1, rows), lax.rem(r + rows - 1, rows)

    barrier = pltpu.get_barrier_semaphore()
    for dy, dz in OFFSETS:
        pl.semaphore_signal(barrier, inc=1, device_id={"col": at(dy, dz)}, device_id_type=MESH)
    for row in (up, down):
        pl.semaphore_signal(barrier, inc=1, device_id={"row": row}, device_id_type=MESH)

    load_diag = pltpu.make_async_copy(ham.at[0, 0], bands.at[0, c], local_sem.at[0])
    load_coupling = pltpu.make_async_copy(ham.at[0, 1], own_ham, local_sem.at[1])
    load_basis = pltpu.make_async_copy(basis, basis_vm, local_sem.at[2])
    load_columns = pltpu.make_async_copy(columns, v0.at[pl.ds(W, rows_here)], local_sem.at[3])
    load_diag.start()
    load_coupling.start()
    load_basis.start()
    load_columns.start()

    row_id = lax.broadcasted_iota(jnp.int32, (8, P_SIZE), 0)
    for k in range(NB):
        peer = at(k // SIDE, k % SIDE)
        first, second = jnp.int32(ENTRIES), jnp.int32(ENTRIES)
        for e in reversed(range(ENTRIES)):
            named = peers[e] == peer
            second = jnp.where(named, first, second)
            first = jnp.where(named, jnp.int32(e), first)
        wanted = []
        for s, found in enumerate((first, second)):
            entry = jnp.minimum(found, ENTRIES - 1)
            live = (found < ENTRIES) & (lax.rem(entry, SLOTS) < tile_count[lax.div(entry, SLOTS)])
            wanted.append(jnp.where(live, tile_block[entry], -1))
            owner[s * NB + k] = entry
            request[s * NB + k] = wanted[s]
        words = jnp.where(row_id == 0, wanted[0], wanted[1])
        if k == 0:
            meta_in[0] = words
        else:
            meta_out[k] = words

    load_coupling.wait()
    bands[1, c] = (own_ham[...].astype(jnp.float32) * pattern[0].astype(jnp.float32)).astype(jnp.bfloat16)
    load_diag.wait()
    pl.semaphore_wait(barrier, NB - 1 + 2)

    def band_copy(half, dy, dz):
        first, second = (dz, dy) if half == 0 else (dy, dz)
        done, hop = (first, second) if second else (0, first)
        before = 0
        if second == 2:
            hop, before = (1, 1) if first < 2 else (-1, -1)
        if half == 0:
            source, there = at(-before, -done), (at(hop, 0) if second else at(0, hop))
        else:
            source, there = at(-done, -before), (at(0, hop) if second else at(hop, 0))
        i = half * (NB - 1) + dy * SIDE + dz - 1
        return remote(bands.at[half, source], bands.at[half, source], band_send.at[i], band_recv.at[i], col=there)

    def band_wait(half, dy, dz):
        i = half * (NB - 1) + dy * SIDE + dz - 1
        block = bands.at[half, at(-dy, -dz)]
        remote(block, block, band_send.at[i], band_recv.at[i], col=at(dy, dz)).wait_recv()

    for d in range(1, SIDE):
        band_copy(0, 0, d).start()
        band_copy(1, d, 0).start()
    halo_up = [remote(columns.at[pl.ds(rows_here - W, W)], v0.at[pl.ds(0, W)], halo_send.at[0], halo_recv.at[0], row=up)]
    halo_down = [remote(columns.at[pl.ds(0, W)], v0.at[pl.ds(rows_here + W, W)], halo_send.at[1], halo_recv.at[1], row=down)]
    for degree, v in ((1, v1), (2, v2)):
        halo_up.append(
            remote(v.at[pl.ds(rows_here, W)], v.at[pl.ds(0, W)], halo_send.at[2 * degree], halo_recv.at[2 * degree], row=up)
        )
        halo_down.append(
            remote(
                v.at[pl.ds(W, W)],
                v.at[pl.ds(rows_here + W, W)],
                halo_send.at[2 * degree + 1],
                halo_recv.at[2 * degree + 1],
                row=down,
            )
        )
    halo_up[0].start()
    halo_down[0].start()
    meta_copies = [
        remote(meta_out.at[k], meta_in.at[k], meta_send.at[k], meta_recv.at[k], col=at(k // SIDE, k % SIDE))
        for k in range(1, NB)
    ]
    for copy in meta_copies:
        copy.start()

    load_basis.wait()
    for s in range(CAP):
        incoming[s * NB] = basis_vm[owner[s * NB]]

        def pack(k, carry, s=s):
            outgoing[s * NB + k] = basis_vm[owner[s * NB + k]]
            return carry

        lax.fori_loop(1, NB, pack, 0)

    for d in range(SIDE):
        if d:
            band_wait(0, 0, d)
            band_wait(1, d, 0)
        for other in (1, SIDE - 1):
            band_copy(0, other, d).start()
            band_copy(1, d, other).start()

    part = 2 * KB // PIECES
    pieces = [(s, half, first) for s in range(CAP) for half in range(2) for first in range(0, KB, part)]

    def send_pieces(s, half, first):
        for dy, dz in OFFSETS:
            i = s * NB + dy * SIDE + dz
            remote(
                outgoing.at[i, half, pl.ds(first, part)],
                incoming.at[i, half, pl.ds(first, part)],
                basis_send.at[i],
                basis_recv.at[i],
                col=at(dy, dz),
            ).start()

    for piece in pieces[:1]:
        send_pieces(*piece)
    for d in range(SIDE):
        near = 1 if d < 2 else SIDE - 1
        band_wait(0, near, d)
        band_copy(0, 2, d).start()
        band_wait(1, d, near)
        band_copy(1, d, 2).start()
    for piece in pieces[1:]:
        send_pieces(*piece)

    for first in range(SIDE):
        for second in (2, SIDE - 1 if first < 2 else 1):
            band_wait(0, second, first)
            band_wait(1, first, second)

    row_at = lax.broadcasted_iota(jnp.int32, (W, W), 0)
    col_at = lax.broadcasted_iota(jnp.int32, (W, W), 1)

    def build(j, carry):
        coupling = bands[1, j].astype(jnp.float32)
        first = jnp.where((j == 0) & (r == 0), 0.0, 1.0)
        last = jnp.where((j == NB - 1) & (r == rows - 1), 0.0, 1.0)
        band[j, :, 0:W] = (jnp.where(col_at >= row_at, coupling, 0.0) * first).astype(jnp.bfloat16)
        band[j, :, W : 2 * W] = bands[0, j]
        band[j, :, 2 * W : 3 * W] = (jnp.where(col_at < row_at, coupling, 0.0) * last).astype(jnp.bfloat16)
        return carry

    lax.fori_loop(0, NB, build, 0)

    def apply(j, v):
        window = v[pl.ds(pl.multiple_of(j * W, W), 3 * W), :]
        return jnp.dot(band[j], window, preferred_element_type=jnp.float32)

    def inner(j):
        return pl.ds(pl.multiple_of((j + 1) * W, W), W)

    def degree_1(j, carry):
        value = apply(j, v0)
        total[j] = value
        v1[inner(j), :] = value.astype(jnp.bfloat16)
        return carry

    c0, c1, c2, c3 = (coef[i] for i in range(4))

    def degree_2(j, carry):
        start = v0[inner(j), :].astype(jnp.float32)
        value = 2.0 * apply(j, v1) - start
        v2[inner(j), :] = value.astype(jnp.bfloat16)
        total[j] = c0 * start + (c1 - c3) * total[j] + c2 * value
        return carry

    def degree_3(j, carry):
        value = total[j] + (2.0 * c3) * apply(j, v2)
        kern[j // 2, pl.ds(pl.multiple_of(lax.rem(j, 2) * W, W), W), :] = value.astype(jnp.bfloat16)
        return carry

    load_columns.wait()
    halo_up[0].wait()
    halo_down[0].wait()
    for step, degree in ((degree_1, 1), (degree_2, 2)):
        step(0, 0)
        step(NB - 1, 0)
        lax.fori_loop(1, NB // 2, step, 0)
        halo_up[degree].start()
        halo_down[degree].start()
        lax.fori_loop(NB // 2, NB - 1, step, 0)
        halo_up[degree].wait()
        halo_down[degree].wait()
    lax.fori_loop(0, NB, degree_3, 0)

    for copy in meta_copies:
        copy.wait()
    meta_copy = pltpu.make_async_copy(meta_in, meta_sm, local_sem.at[4])
    meta_copy.start()
    meta_copy.wait()
    for s in range(CAP):
        for k in range(NB):
            block_of[s * NB + k] = meta_sm[k, s, 0]

    def basis_copy(i):
        return remote(outgoing.at[i], incoming.at[i], basis_send.at[i], basis_recv.at[i], col=at(0, 1))

    def project(s, k):
        i = s * NB + k
        keep = pltpu.make_async_copy(incoming.at[i], received.at[i], out_sem.at[i])
        keep.start()
        block = jnp.maximum(meta_sm[k, s, 0], 0)
        product = jnp.dot(kern[block], incoming[i, 1], preferred_element_type=jnp.float32)
        return jnp.sum(product * incoming[i, 0].astype(jnp.float32), axis=0, keepdims=True) * (1.0 / KB)

    for s in range(CAP):
        contrib_in[0, s : s + 1, :] = project(s, 0)

        def step(k, carry, s=s):
            basis_copy(s * NB + k).wait_recv()
            contrib_out[k, s : s + 1, :] = project(s, k)
            return carry

        lax.fori_loop(1, NB, step, 0)

    contrib_copies = [
        remote(
            contrib_out.at[k],
            contrib_in.at[k],
            contrib_send.at[k],
            contrib_recv.at[k],
            col=at(-(k // SIDE), -(k % SIDE)),
        )
        for k in range(1, NB)
    ]
    for copy in contrib_copies:
        copy.start()
    for copy in contrib_copies:
        copy.wait()

    potentials = []
    for t in range(ENTRIES // SLOTS):
        density = core[t : t + 1, :]
        for slot in range(SLOTS):
            e = t * SLOTS + slot
            there = peers[e]
            k = lax.rem(lax.div(there, SIDE) + SIDE - y, SIDE) * SIDE + lax.rem(lax.rem(there, SIDE) + SIDE - z, SIDE)
            both = contrib_in[k]
            mine = jnp.where(owner[k] == e, both[0:1], both[1:2])
            density = density + jnp.where(slot < tile_count[t], mine, 0.0)
        dens[t : t + 1, :] = density
        x = jnp.maximum(density, 0.1)
        root = jnp.exp(jnp.log(x) * (1.0 / 3.0))
        root = root - (root * root * root - x) / (3.0 * root * root)
        potentials.append(-exchange_factor * root)

    for k in range(NB):
        lines = []
        for s in range(CAP):
            tile = lax.div(owner[s * NB + k], SLOTS)
            line = potentials[0]
            for t in range(1, ENTRIES // SLOTS):
                line = jnp.where(tile == t, potentials[t], line)
            lines.append(jnp.where(request[s * NB + k] >= 0, line, 0.0))
        words = jnp.where(row_id == 0, lines[0], lines[1])
        if k == 0:
            pot_got[0] = words
        else:
            pot_out[k] = words
    pot_copies = [
        remote(pot_out.at[k], pot_got.at[k], pot_send.at[k], pot_recv.at[k], col=at(k // SIDE, k % SIDE))
        for k in range(1, NB)
    ]
    for copy in pot_copies:
        copy.start()
    for half in range(2):
        for dy, dz in OFFSETS:
            band_copy(half, dy, dz).wait_send()

    def finish(k, carry):
        for s in range(CAP):
            basis_copy(s * NB + k).wait_send()
        return carry

    lax.fori_loop(1, NB, finish, 0)

    def kept(i, carry):
        pltpu.make_async_copy(incoming.at[i], received.at[i], out_sem.at[i]).wait()
        return carry

    lax.fori_loop(0, CAP * NB, kept, 0)
    for copy in pot_copies:
        copy.wait()
    pot_in[...] = pot_got[...]


def exchange(columns, ham, pattern, coef, peers, tile_block, tile_count, basis, core):
    any_spec = pl.BlockSpec(memory_space=pl.ANY)
    smem = pl.BlockSpec(memory_space=pltpu.SMEM)
    vmem = pl.BlockSpec(memory_space=pltpu.VMEM)
    rows_here = NB * W
    slots = CAP * NB
    bf16, f32, i32 = jnp.bfloat16, jnp.float32, jnp.int32
    dma = pltpu.SemaphoreType.DMA
    return pl.pallas_call(
        exchange_kernel,
        out_shape=(
            jax.ShapeDtypeStruct(core.shape, f32),
            jax.ShapeDtypeStruct((slots, 2, KB, P_SIZE), bf16),
            jax.ShapeDtypeStruct((NB, 8, P_SIZE), f32),
            jax.ShapeDtypeStruct((slots,), i32),
        ),
        in_specs=[any_spec, any_spec, smem, smem, smem, smem, smem, any_spec, vmem],
        out_specs=(vmem, any_spec, vmem, smem),
        scratch_shapes=[
            pltpu.VMEM((W, W), bf16),
            pltpu.VMEM((2, NB, W, W), bf16),
            pltpu.VMEM((NB, W, 3 * W), bf16),
            pltpu.VMEM((rows_here + 2 * W, KB), bf16),
            pltpu.VMEM((rows_here + 2 * W, KB), bf16),
            pltpu.VMEM((rows_here + 2 * W, KB), bf16),
            pltpu.VMEM((NB, W, KB), f32),
            pltpu.VMEM((rows_here // KB, KB, KB), bf16),
            pltpu.VMEM(basis.shape, bf16),
            pltpu.VMEM((slots, 2, KB, P_SIZE), bf16),
            pltpu.VMEM((slots, 2, KB, P_SIZE), bf16),
            pltpu.VMEM((NB, 8, P_SIZE), i32),
            pltpu.VMEM((NB, 8, P_SIZE), i32),
            pltpu.SMEM((NB, 8, P_SIZE), i32),
            pltpu.VMEM((NB, 8, P_SIZE), f32),
            pltpu.VMEM((NB, 8, P_SIZE), f32),
            pltpu.VMEM((NB, 8, P_SIZE), f32),
            pltpu.VMEM((NB, 8, P_SIZE), f32),
            pltpu.SMEM((slots,), i32),
            pltpu.SMEM((slots,), i32),
            dma((5,)),
            dma((slots,)),
            dma((2 * (NB - 1),)),
            dma((2 * (NB - 1),)),
            dma((NB,)),
            dma((NB,)),
            dma((6,)),
            dma((6,)),
            dma((slots,)),
            dma((slots,)),
            dma((NB,)),
            dma((NB,)),
            dma((NB,)),
            dma((NB,)),
        ],
        compiler_params=pltpu.CompilerParams(
            collective_id=0, has_side_effects=True, vmem_limit_bytes=66_000_000
        ),
        name="exchange",
    )(columns, ham, pattern, coef, peers, tile_block, tile_count, basis, core)


def update_kernel(received, pot, block_of, out, pairs, lines, blocks, total, rounded, pair_sem, sem):
    slots = CAP * NB
    load_blocks = pltpu.make_async_copy(block_of, blocks, sem.at[0])
    load_lines = pltpu.make_async_copy(pot, lines, sem.at[1])
    load_blocks.start()
    load_lines.start()
    load_blocks.wait()

    def load(i):
        return pltpu.make_async_copy(received.at[i], pairs.at[i], pair_sem.at[i])

    def fetch(i, carry):
        @pl.when(blocks[i] >= 0)
        def _():
            load(i).start()

        return carry

    lax.fori_loop(0, slots, fetch, 0)
    total[...] = jnp.zeros_like(total)
    load_lines.wait()

    def add(i, carry):
        block = blocks[i]

        @pl.when(block >= 0)
        def _():
            load(i).wait()
            both = lines[lax.rem(i, NB)]
            line = jnp.where(i < NB, both[0:1], both[1:2])
            weighted = (pairs[i, 1].astype(jnp.float32) * line).astype(jnp.bfloat16)
            product = lax.dot_general(
                pairs[i, 0], weighted, (((1,), (1,)), ((), ())), preferred_element_type=jnp.float32
            )
            product = (product * (1.0 / math.sqrt(P_SIZE))).astype(jnp.bfloat16).astype(jnp.float32)
            total[block] = total[block] + product

        return carry

    lax.fori_loop(0, slots, add, 0)

    def store(b):
        return pltpu.make_async_copy(rounded.at[b], out.at[b], sem.at[2 + b])

    for b in range(NB * W // KB):
        rounded[b] = total[b].astype(jnp.bfloat16)
        store(b).start()
    for b in range(NB * W // KB):
        store(b).wait()


def update(block_of, received, pot_in):
    blocks = NB * W // KB
    any_spec = pl.BlockSpec(memory_space=pl.ANY)
    return pl.pallas_call(
        update_kernel,
        out_shape=jax.ShapeDtypeStruct((blocks, KB, KB), jnp.bfloat16),
        in_specs=[any_spec, any_spec, any_spec],
        out_specs=any_spec,
        scratch_shapes=[
            pltpu.VMEM(received.shape, received.dtype),
            pltpu.VMEM(pot_in.shape, pot_in.dtype),
            pltpu.SMEM(block_of.shape, block_of.dtype),
            pltpu.VMEM((blocks, KB, KB), jnp.float32),
            pltpu.VMEM((blocks, KB, KB), jnp.bfloat16),
            pltpu.SemaphoreType.DMA((CAP * NB,)),
            pltpu.SemaphoreType.DMA((2 + blocks,)),
        ],
        compiler_params=pltpu.CompilerParams(vmem_limit_bytes=67_000_000),
        name="update",
    )(received, pot_in, block_of)


def shards(columns, ham, pattern, coef, peers, tile_block, tile_count, basis, core):
    dens, received, pot_in, block_of = exchange(
        columns, ham, pattern, coef, peers.reshape(-1), tile_block, tile_count, basis, core
    )
    blocks = update(block_of, received, pot_in)
    return dens, blocks.reshape(columns.shape)


def solution(mesh):
    return jax.shard_map(
        shards,
        mesh=mesh,
        in_specs=(
            P("row", "col"),
            P(("row", "col"), None, None, None),
            P(("row", "col")),
            P(),
            P(("row", "col"), None),
            P(("row", "col")),
            P(("row", "col")),
            P(("row", "col"), None, None, None),
            P(("row", "col"), None),
        ),
        out_specs=(P(("row", "col"), None), P("row", "col")),
        check_vma=False,
    )
```

```python
import functools
import math

import jax
import jax.numpy as jnp
from jax import lax
from jax.experimental import pallas as pl
from jax.experimental.pallas import tpu as pltpu
from jax.sharding import PartitionSpec as P

MESH = pl.DeviceIdType.MESH
W = 256
KB = 512
SLOTS = 4
CAP = 2
P_SIZE = 128
NB = 16
ENTRIES = 16
PIECES = 8
SIDE = 4
OFFSETS = tuple((k // SIDE, k % SIDE) for k in range(1, NB))

exchange_factor = (3.0 / math.pi) ** (1.0 / 3.0)


def exchange_kernel(
    columns,
    ham,
    pattern,
    coef,
    peers,
    tile_block,
    tile_count,
    basis,
    core,
    dens,
    received,
    pot_in,
    block_of,
    own_ham,
    bands,
    band,
    v0,
    v1,
    v2,
    total,
    kern,
    basis_vm,
    outgoing,
    incoming,
    meta_out,
    meta_in,
    meta_sm,
    contrib_out,
    contrib_in,
    pot_out,
    pot_got,
    owner,
    request,
    local_sem,
    out_sem,
    band_send,
    band_recv,
    meta_send,
    meta_recv,
    halo_send,
    halo_recv,
    basis_send,
    basis_recv,
    contrib_send,
    contrib_recv,
    pot_send,
    pot_recv,
):
    r = lax.axis_index("row")
    c = lax.axis_index("col")
    rows = lax.axis_size("row")
    y, z = c // SIDE, c % SIDE
    rows_here = NB * W

    def at(dy, dz):
        return lax.rem(y + dy + SIDE, SIDE) * SIDE + lax.rem(z + dz + SIDE, SIDE)

    def remote(src, dst, send, recv, **where):
        return pltpu.make_async_remote_copy(
            src_ref=src, dst_ref=dst, send_sem=send, recv_sem=recv, device_id=where, device_id_type=MESH
        )

    up, down = lax.rem(r + 1, rows), lax.rem(r + rows - 1, rows)

    barrier = pltpu.get_barrier_semaphore()
    for dy, dz in OFFSETS:
        pl.semaphore_signal(barrier, inc=1, device_id={"col": at(dy, dz)}, device_id_type=MESH)
    for row in (up, down):
        pl.semaphore_signal(barrier, inc=1, device_id={"row": row}, device_id_type=MESH)

    load_diag = pltpu.make_async_copy(ham.at[0, 0], bands.at[0, c], local_sem.at[0])
    load_coupling = pltpu.make_async_copy(ham.at[0, 1], own_ham, local_sem.at[1])
    load_basis = pltpu.make_async_copy(basis, basis_vm, local_sem.at[2])
    load_columns = pltpu.make_async_copy(columns, v0.at[pl.ds(W, rows_here)], local_sem.at[3])
    load_diag.start()
    load_coupling.start()
    load_basis.start()
    load_columns.start()

    row_id = lax.broadcasted_iota(jnp.int32, (8, P_SIZE), 0)
    for k in range(NB):
        peer = at(k // SIDE, k % SIDE)
        first, second = jnp.int32(ENTRIES), jnp.int32(ENTRIES)
        for e in reversed(range(ENTRIES)):
            named = peers[e] == peer
            second = jnp.where(named, first, second)
            first = jnp.where(named, jnp.int32(e), first)
        wanted = []
        for s, found in enumerate((first, second)):
            entry = jnp.minimum(found, ENTRIES - 1)
            live = (found < ENTRIES) & (lax.rem(entry, SLOTS) < tile_count[lax.div(entry, SLOTS)])
            wanted.append(jnp.where(live, tile_block[entry], -1))
            owner[s * NB + k] = entry
            request[s * NB + k] = wanted[s]
        words = jnp.where(row_id == 0, wanted[0], wanted[1])
        if k == 0:
            meta_in[0] = words
        else:
            meta_out[k] = words

    load_coupling.wait()
    bands[1, c] = (own_ham[...].astype(jnp.float32) * pattern[0].astype(jnp.float32)).astype(jnp.bfloat16)
    load_diag.wait()
    pl.semaphore_wait(barrier, NB - 1 + 2)

    def band_copy(half, dy, dz):
        first, second = (dz, dy) if half == 0 else (dy, dz)
        done, hop = (first, second) if second else (0, first)
        before = 0
        if second == 2:
            hop, before = (1, 1) if first < 2 else (-1, -1)
        if half == 0:
            source, there = at(-before, -done), (at(hop, 0) if second else at(0, hop))
        else:
            source, there = at(-done, -before), (at(0, hop) if second else at(hop, 0))
        i = half * (NB - 1) + dy * SIDE + dz - 1
        return remote(bands.at[half, source], bands.at[half, source], band_send.at[i], band_recv.at[i], col=there)

    def band_wait(half, dy, dz):
        i = half * (NB - 1) + dy * SIDE + dz - 1
        block = bands.at[half, at(-dy, -dz)]
        remote(block, block, band_send.at[i], band_recv.at[i], col=at(dy, dz)).wait_recv()

    for d in range(1, SIDE):
        band_copy(0, 0, d).start()
        band_copy(1, d, 0).start()
    halo_up = [remote(columns.at[pl.ds(rows_here - W, W)], v0.at[pl.ds(0, W)], halo_send.at[0], halo_recv.at[0], row=up)]
    halo_down = [remote(columns.at[pl.ds(0, W)], v0.at[pl.ds(rows_here + W, W)], halo_send.at[1], halo_recv.at[1], row=down)]
    for degree, v in ((1, v1), (2, v2)):
        halo_up.append(
            remote(v.at[pl.ds(rows_here, W)], v.at[pl.ds(0, W)], halo_send.at[2 * degree], halo_recv.at[2 * degree], row=up)
        )
        halo_down.append(
            remote(
                v.at[pl.ds(W, W)],
                v.at[pl.ds(rows_here + W, W)],
                halo_send.at[2 * degree + 1],
                halo_recv.at[2 * degree + 1],
                row=down,
            )
        )
    halo_up[0].start()
    halo_down[0].start()
    meta_copies = [
        remote(meta_out.at[k], meta_in.at[k], meta_send.at[k], meta_recv.at[k], col=at(k // SIDE, k % SIDE))
        for k in range(1, NB)
    ]
    for copy in meta_copies:
        copy.start()

    load_basis.wait()
    for s in range(CAP):
        incoming[s * NB] = basis_vm[owner[s * NB]]

        def pack(k, carry, s=s):
            outgoing[s * NB + k] = basis_vm[owner[s * NB + k]]
            return carry

        lax.fori_loop(1, NB, pack, 0)

    for d in range(SIDE):
        if d:
            band_wait(0, 0, d)
            band_wait(1, d, 0)
        for other in (1, SIDE - 1):
            band_copy(0, other, d).start()
            band_copy(1, d, other).start()

    part = 2 * KB // PIECES
    pieces = [(s, half, first) for s in range(CAP) for half in range(2) for first in range(0, KB, part)]

    def send_pieces(s, half, first):
        for dy, dz in OFFSETS:
            i = s * NB + dy * SIDE + dz
            remote(
                outgoing.at[i, half, pl.ds(first, part)],
                incoming.at[i, half, pl.ds(first, part)],
                basis_send.at[i],
                basis_recv.at[i],
                col=at(dy, dz),
            ).start()

    for piece in pieces[:1]:
        send_pieces(*piece)
    for d in range(SIDE):
        near = 1 if d < 2 else SIDE - 1
        band_wait(0, near, d)
        band_copy(0, 2, d).start()
        band_wait(1, d, near)
        band_copy(1, d, 2).start()
    for piece in pieces[1:]:
        send_pieces(*piece)

    for first in range(SIDE):
        for second in (2, SIDE - 1 if first < 2 else 1):
            band_wait(0, second, first)
            band_wait(1, first, second)

    row_at = lax.broadcasted_iota(jnp.int32, (W, W), 0)
    col_at = lax.broadcasted_iota(jnp.int32, (W, W), 1)

    def build(j, carry):
        coupling = bands[1, j].astype(jnp.float32)
        first = jnp.where((j == 0) & (r == 0), 0.0, 1.0)
        last = jnp.where((j == NB - 1) & (r == rows - 1), 0.0, 1.0)
        band[j, :, 0:W] = (jnp.where(col_at >= row_at, coupling, 0.0) * first).astype(jnp.bfloat16)
        band[j, :, W : 2 * W] = bands[0, j]
        band[j, :, 2 * W : 3 * W] = (jnp.where(col_at < row_at, coupling, 0.0) * last).astype(jnp.bfloat16)
        return carry

    lax.fori_loop(0, NB, build, 0)

    def apply(j, v):
        window = v[pl.ds(pl.multiple_of(j * W, W), 3 * W), :]
        return jnp.dot(band[j], window, preferred_element_type=jnp.float32)

    def inner(j):
        return pl.ds(pl.multiple_of((j + 1) * W, W), W)

    def degree_1(j, carry):
        value = apply(j, v0)
        total[j] = value
        v1[inner(j), :] = value.astype(jnp.bfloat16)
        return carry

    c0, c1, c2, c3 = (coef[i] for i in range(4))

    def degree_2(j, carry):
        start = v0[inner(j), :].astype(jnp.float32)
        value = 2.0 * apply(j, v1) - start
        v2[inner(j), :] = value.astype(jnp.bfloat16)
        total[j] = c0 * start + (c1 - c3) * total[j] + c2 * value
        return carry

    def degree_3(j, carry):
        value = total[j] + (2.0 * c3) * apply(j, v2)
        kern[j // 2, pl.ds(pl.multiple_of(lax.rem(j, 2) * W, W), W), :] = value.astype(jnp.bfloat16)
        return carry

    load_columns.wait()
    halo_up[0].wait()
    halo_down[0].wait()
    for step, degree in ((degree_1, 1), (degree_2, 2)):
        step(0, 0)
        step(NB - 1, 0)
        lax.fori_loop(1, NB // 2, step, 0)
        halo_up[degree].start()
        halo_down[degree].start()
        lax.fori_loop(NB // 2, NB - 1, step, 0)
        halo_up[degree].wait()
        halo_down[degree].wait()
    lax.fori_loop(0, NB, degree_3, 0)

    for copy in meta_copies:
        copy.wait()
    meta_copy = pltpu.make_async_copy(meta_in, meta_sm, local_sem.at[4])
    meta_copy.start()
    meta_copy.wait()
    for s in range(CAP):
        for k in range(NB):
            block_of[s * NB + k] = meta_sm[k, s, 0]

    def basis_copy(i):
        return remote(outgoing.at[i], incoming.at[i], basis_send.at[i], basis_recv.at[i], col=at(0, 1))

    def project(s, k):
        i = s * NB + k
        keep = pltpu.make_async_copy(incoming.at[i], received.at[i], out_sem.at[i])
        keep.start()
        block = jnp.maximum(meta_sm[k, s, 0], 0)
        product = jnp.dot(kern[block], incoming[i, 1], preferred_element_type=jnp.float32)
        return jnp.sum(product * incoming[i, 0].astype(jnp.float32), axis=0, keepdims=True) * (1.0 / KB)

    for s in range(CAP):
        contrib_in[0, s : s + 1, :] = project(s, 0)

        def step(k, carry, s=s):
            basis_copy(s * NB + k).wait_recv()
            contrib_out[k, s : s + 1, :] = project(s, k)
            return carry

        lax.fori_loop(1, NB, step, 0)

    contrib_copies = [
        remote(
            contrib_out.at[k],
            contrib_in.at[k],
            contrib_send.at[k],
            contrib_recv.at[k],
            col=at(-(k // SIDE), -(k % SIDE)),
        )
        for k in range(1, NB)
    ]
    for copy in contrib_copies:
        copy.start()
    for copy in contrib_copies:
        copy.wait()

    potentials = []
    for t in range(ENTRIES // SLOTS):
        density = core[t : t + 1, :]
        for slot in range(SLOTS):
            e = t * SLOTS + slot
            there = peers[e]
            k = lax.rem(lax.div(there, SIDE) + SIDE - y, SIDE) * SIDE + lax.rem(lax.rem(there, SIDE) + SIDE - z, SIDE)
            both = contrib_in[k]
            mine = jnp.where(owner[k] == e, both[0:1], both[1:2])
            density = density + jnp.where(slot < tile_count[t], mine, 0.0)
        dens[t : t + 1, :] = density
        x = jnp.maximum(density, 0.1)
        root = jnp.exp(jnp.log(x) * (1.0 / 3.0))
        root = root - (root * root * root - x) / (3.0 * root * root)
        potentials.append(-exchange_factor * root)

    for k in range(NB):
        lines = []
        for s in range(CAP):
            tile = lax.div(owner[s * NB + k], SLOTS)
            line = potentials[0]
            for t in range(1, ENTRIES // SLOTS):
                line = jnp.where(tile == t, potentials[t], line)
            lines.append(jnp.where(request[s * NB + k] >= 0, line, 0.0))
        words = jnp.where(row_id == 0, lines[0], lines[1])
        if k == 0:
            pot_got[0] = words
        else:
            pot_out[k] = words
    pot_copies = [
        remote(pot_out.at[k], pot_got.at[k], pot_send.at[k], pot_recv.at[k], col=at(k // SIDE, k % SIDE))
        for k in range(1, NB)
    ]
    for copy in pot_copies:
        copy.start()
    for half in range(2):
        for dy, dz in OFFSETS:
            band_copy(half, dy, dz).wait_send()

    def finish(k, carry):
        for s in range(CAP):
            basis_copy(s * NB + k).wait_send()
        return carry

    lax.fori_loop(1, NB, finish, 0)

    def kept(i, carry):
        pltpu.make_async_copy(incoming.at[i], received.at[i], out_sem.at[i]).wait()
        return carry

    lax.fori_loop(0, CAP * NB, kept, 0)
    for copy in pot_copies:
        copy.wait()
    pot_in[...] = pot_got[...]


def exchange(columns, ham, pattern, coef, peers, tile_block, tile_count, basis, core):
    any_spec = pl.BlockSpec(memory_space=pl.ANY)
    smem = pl.BlockSpec(memory_space=pltpu.SMEM)
    vmem = pl.BlockSpec(memory_space=pltpu.VMEM)
    rows_here = NB * W
    slots = CAP * NB
    bf16, f32, i32 = jnp.bfloat16, jnp.float32, jnp.int32
    dma = pltpu.SemaphoreType.DMA
    return pl.pallas_call(
        exchange_kernel,
        out_shape=(
            jax.ShapeDtypeStruct(core.shape, f32),
            jax.ShapeDtypeStruct((slots, 2, KB, P_SIZE), bf16),
            jax.ShapeDtypeStruct((NB, 8, P_SIZE), f32),
            jax.ShapeDtypeStruct((slots,), i32),
        ),
        in_specs=[any_spec, any_spec, smem, smem, smem, smem, smem, any_spec, vmem],
        out_specs=(vmem, any_spec, vmem, smem),
        scratch_shapes=[
            pltpu.VMEM((W, W), bf16),
            pltpu.VMEM((2, NB, W, W), bf16),
            pltpu.VMEM((NB, W, 3 * W), bf16),
            pltpu.VMEM((rows_here + 2 * W, KB), bf16),
            pltpu.VMEM((rows_here + 2 * W, KB), bf16),
            pltpu.VMEM((rows_here + 2 * W, KB), bf16),
            pltpu.VMEM((NB, W, KB), f32),
            pltpu.VMEM((rows_here // KB, KB, KB), bf16),
            pltpu.VMEM(basis.shape, bf16),
            pltpu.VMEM((slots, 2, KB, P_SIZE), bf16),
            pltpu.VMEM((slots, 2, KB, P_SIZE), bf16),
            pltpu.VMEM((NB, 8, P_SIZE), i32),
            pltpu.VMEM((NB, 8, P_SIZE), i32),
            pltpu.SMEM((NB, 8, P_SIZE), i32),
            pltpu.VMEM((NB, 8, P_SIZE), f32),
            pltpu.VMEM((NB, 8, P_SIZE), f32),
            pltpu.VMEM((NB, 8, P_SIZE), f32),
            pltpu.VMEM((NB, 8, P_SIZE), f32),
            pltpu.SMEM((slots,), i32),
            pltpu.SMEM((slots,), i32),
            dma((5,)),
            dma((slots,)),
            dma((2 * (NB - 1),)),
            dma((2 * (NB - 1),)),
            dma((NB,)),
            dma((NB,)),
            dma((6,)),
            dma((6,)),
            dma((slots,)),
            dma((slots,)),
            dma((NB,)),
            dma((NB,)),
            dma((NB,)),
            dma((NB,)),
        ],
        compiler_params=pltpu.CompilerParams(
            collective_id=0, has_side_effects=True, vmem_limit_bytes=66_000_000
        ),
        name="exchange",
    )(columns, ham, pattern, coef, peers, tile_block, tile_count, basis, core)


def update_kernel(received, pot, block_of, out, pairs, lines, blocks, named, count, total, rounded, pair_sem, sem):
    slots = CAP * NB
    row_blocks = NB * W // KB
    load_blocks = pltpu.make_async_copy(block_of, blocks, sem.at[0])
    load_lines = pltpu.make_async_copy(pot, lines, sem.at[1])
    load_blocks.start()
    load_lines.start()
    for b in range(row_blocks):
        count[b] = 0
    load_blocks.wait()

    def load(i):
        return pltpu.make_async_copy(received.at[i], pairs.at[i], pair_sem.at[i])

    def sort(i, carry):
        block = blocks[i]

        @pl.when(block >= 0)
        def _():
            named[block * slots + count[block]] = i
            count[block] = count[block] + 1

        return carry

    lax.fori_loop(0, slots, sort, 0)

    def fetch(b, carry):
        def one(j, carry):
            load(named[b * slots + j]).start()
            return carry

        return lax.fori_loop(0, count[b], one, carry)

    lax.fori_loop(0, row_blocks, fetch, 0)
    load_lines.wait()

    def store(b):
        return pltpu.make_async_copy(rounded.at[b], out.at[b], sem.at[2 + b])

    def weighted(i, present):
        both = lines[lax.rem(i, NB)]
        line = jnp.where(i < NB, both[0:1], both[1:2])
        line = jnp.where(present, line, 0.0)
        return (pairs[i, 1].astype(jnp.float32) * line).astype(jnp.bfloat16)

    def block_sum(b, carry):
        n = count[b]

        def add(j, carry):
            first = named[b * slots + 2 * j]
            paired = 2 * j + 1 < n
            second = jnp.where(paired, named[b * slots + 2 * j + 1], first)
            load(first).wait()

            @pl.when(paired)
            def _():
                load(second).wait()

            left = jnp.concatenate([pairs[first, 0], pairs[second, 0]], axis=1)
            right = jnp.concatenate([weighted(first, True), weighted(second, paired)], axis=1)
            product = lax.dot_general(left, right, (((1,), (1,)), ((), ())), preferred_element_type=jnp.float32)

            @pl.when(j == 0)
            def _():
                total[...] = product

            @pl.when(j > 0)
            def _():
                total[...] = total[...] + product

            return carry

        lax.fori_loop(0, lax.div(n + 1, 2), add, 0)
        value = jnp.where(n > 0, total[...] * (1.0 / math.sqrt(P_SIZE)), 0.0)
        rounded[b] = value.astype(jnp.bfloat16)
        store(b).start()
        return carry

    lax.fori_loop(0, row_blocks, block_sum, 0)
    for b in range(row_blocks):
        store(b).wait()


def update(block_of, received, pot_in):
    blocks = NB * W // KB
    any_spec = pl.BlockSpec(memory_space=pl.ANY)
    return pl.pallas_call(
        update_kernel,
        out_shape=jax.ShapeDtypeStruct((blocks, KB, KB), jnp.bfloat16),
        in_specs=[any_spec, any_spec, any_spec],
        out_specs=any_spec,
        scratch_shapes=[
            pltpu.VMEM(received.shape, received.dtype),
            pltpu.VMEM(pot_in.shape, pot_in.dtype),
            pltpu.SMEM(block_of.shape, block_of.dtype),
            pltpu.SMEM((blocks * CAP * NB,), jnp.int32),
            pltpu.SMEM((blocks,), jnp.int32),
            pltpu.VMEM((KB, KB), jnp.float32),
            pltpu.VMEM((blocks, KB, KB), jnp.bfloat16),
            pltpu.SemaphoreType.DMA((CAP * NB,)),
            pltpu.SemaphoreType.DMA((2 + blocks,)),
        ],
        compiler_params=pltpu.CompilerParams(vmem_limit_bytes=67_000_000),
        name="update",
    )(received, pot_in, block_of)


def shards(columns, ham, pattern, coef, peers, tile_block, tile_count, basis, core):
    dens, received, pot_in, block_of = exchange(
        columns, ham, pattern, coef, peers.reshape(-1), tile_block, tile_count, basis, core
    )
    blocks = update(block_of, received, pot_in)
    return dens, blocks.reshape(columns.shape)


def solution(mesh):
    return jax.shard_map(
        shards,
        mesh=mesh,
        in_specs=(
            P("row", "col"),
            P(("row", "col"), None, None, None),
            P(("row", "col")),
            P(),
            P(("row", "col"), None),
            P(("row", "col")),
            P(("row", "col")),
            P(("row", "col"), None, None, None),
            P(("row", "col"), None),
        ),
        out_specs=(P(("row", "col"), None), P("row", "col")),
        check_vma=False,
    )
```

```python
import functools
import math

import jax
import jax.numpy as jnp
from jax import lax
from jax.experimental import pallas as pl
from jax.experimental.pallas import tpu as pltpu
from jax.sharding import PartitionSpec as P

MESH = pl.DeviceIdType.MESH
W = 256
KB = 512
SLOTS = 4
CAP = 2
P_SIZE = 128
NB = 16
ENTRIES = 16
PIECES = 8
EARLY = 1
SIDE = 4
OFFSETS = tuple((k // SIDE, k % SIDE) for k in range(1, NB))

exchange_factor = (3.0 / math.pi) ** (1.0 / 3.0)


def exchange_kernel(
    columns,
    ham,
    pattern,
    coef,
    peers,
    tile_block,
    tile_count,
    basis,
    core,
    dens,
    received,
    pot_in,
    block_of,
    present,
    own_ham,
    bands,
    band,
    v0,
    v1,
    v2,
    total,
    kern,
    basis_vm,
    outgoing,
    incoming,
    meta_out,
    meta_in,
    meta_sm,
    core_out,
    core_in,
    contrib,
    tile_density,
    owner,
    local_sem,
    out_sem,
    band_send,
    band_recv,
    meta_send,
    meta_recv,
    halo_send,
    halo_recv,
    basis_send,
    basis_recv,
    contrib_send,
    contrib_recv,
    core_send,
    core_recv,
):
    r = lax.axis_index("row")
    c = lax.axis_index("col")
    rows = lax.axis_size("row")
    y, z = c // SIDE, c % SIDE
    rows_here = NB * W

    def at(dy, dz):
        return lax.rem(y + dy + SIDE, SIDE) * SIDE + lax.rem(z + dz + SIDE, SIDE)

    def remote(src, dst, send, recv, **where):
        return pltpu.make_async_remote_copy(
            src_ref=src, dst_ref=dst, send_sem=send, recv_sem=recv, device_id=where, device_id_type=MESH
        )

    up, down = lax.rem(r + 1, rows), lax.rem(r + rows - 1, rows)

    barrier = pltpu.get_barrier_semaphore()
    for dy, dz in OFFSETS:
        pl.semaphore_signal(barrier, inc=1, device_id={"col": at(dy, dz)}, device_id_type=MESH)
    for row in (up, down):
        pl.semaphore_signal(barrier, inc=1, device_id={"row": row}, device_id_type=MESH)

    load_diag = pltpu.make_async_copy(ham.at[0, 0], bands.at[0, c], local_sem.at[0])
    load_coupling = pltpu.make_async_copy(ham.at[0, 1], own_ham, local_sem.at[1])
    load_basis = pltpu.make_async_copy(basis, basis_vm, local_sem.at[2])
    load_columns = pltpu.make_async_copy(columns, v0.at[pl.ds(W, rows_here)], local_sem.at[3])
    load_pattern = pltpu.make_async_copy(pattern, present, local_sem.at[5])
    load_pattern.start()
    load_diag.start()
    load_coupling.start()
    load_basis.start()
    load_columns.start()

    core_out[...] = jnp.concatenate([core[...], jnp.zeros_like(core[...])], axis=0)
    core_in[0] = core_out[...]
    lane = lax.broadcasted_iota(jnp.int32, (8, P_SIZE), 1)
    codes = jnp.full((8, P_SIZE), -1, jnp.int32)
    slots_of = []
    for k in range(NB):
        peer = at(k // SIDE, k % SIDE)
        first, second = jnp.int32(ENTRIES), jnp.int32(ENTRIES)
        for e in reversed(range(ENTRIES)):
            named = peers[e] == peer
            second = jnp.where(named, first, second)
            first = jnp.where(named, jnp.int32(e), first)
        fields = []
        for s, found in enumerate((first, second)):
            entry = jnp.minimum(found, ENTRIES - 1)
            live = (found < ENTRIES) & (lax.rem(entry, SLOTS) < tile_count[lax.div(entry, SLOTS)])
            owner[s * NB + k] = entry
            fields.append((jnp.where(live, tile_block[entry], -1), lax.div(entry, SLOTS)))
            codes = jnp.where((lane == entry) & live, peer * (CAP * NB) + s * NB + k, codes)
        slots_of.append(fields)
    for k in range(NB):
        words = codes
        for s in range(CAP):
            words = jnp.where(lane == ENTRIES + s, slots_of[k][s][0], words)
            words = jnp.where(lane == ENTRIES + CAP + s, slots_of[k][s][1], words)
        if k == 0:
            meta_in[0] = words
        else:
            meta_out[k] = words

    load_pattern.wait()
    load_coupling.wait()
    bands[1, c] = (own_ham[...].astype(jnp.float32) * present[0].astype(jnp.float32)).astype(jnp.bfloat16)
    load_diag.wait()
    pl.semaphore_wait(barrier, NB - 1 + 2)

    def band_copy(half, dy, dz):
        first, second = (dz, dy) if half == 0 else (dy, dz)
        done, hop = (first, second) if second else (0, first)
        before = 0
        if second == 2:
            hop, before = (1, 1) if first < 2 else (-1, -1)
        if half == 0:
            source, there = at(-before, -done), (at(hop, 0) if second else at(0, hop))
        else:
            source, there = at(-done, -before), (at(0, hop) if second else at(hop, 0))
        i = half * (NB - 1) + dy * SIDE + dz - 1
        return remote(bands.at[half, source], bands.at[half, source], band_send.at[i], band_recv.at[i], col=there)

    def band_wait(half, dy, dz):
        i = half * (NB - 1) + dy * SIDE + dz - 1
        block = bands.at[half, at(-dy, -dz)]
        remote(block, block, band_send.at[i], band_recv.at[i], col=at(dy, dz)).wait_recv()

    def band_part(half, side):
        hop = 1 - 2 * side
        along = (lambda step: at(0, step)) if half == 0 else (lambda step: at(step, 0))
        part = bands.at[half, along(-hop), pl.ds(side * (W // 2), W // 2)]
        i = 2 * (NB - 1) + 2 * half + side
        return remote(part, part, band_send.at[i], band_recv.at[i], col=along(hop))

    def band_part_wait(half, side):
        along = (lambda step: at(0, step)) if half == 0 else (lambda step: at(step, 0))
        part = bands.at[half, along(2), pl.ds(side * (W // 2), W // 2)]
        i = 2 * (NB - 1) + 2 * half + side
        remote(part, part, band_send.at[i], band_recv.at[i], col=along(1)).wait_recv()

    for d in (1, SIDE - 1):
        band_copy(0, 0, d).start()
        band_copy(1, d, 0).start()
    halo_up = [remote(columns.at[pl.ds(rows_here - W, W)], v0.at[pl.ds(0, W)], halo_send.at[0], halo_recv.at[0], row=up)]
    halo_down = [remote(columns.at[pl.ds(0, W)], v0.at[pl.ds(rows_here + W, W)], halo_send.at[1], halo_recv.at[1], row=down)]
    for degree, v in ((1, v1), (2, v2)):
        halo_up.append(
            remote(v.at[pl.ds(rows_here, W)], v.at[pl.ds(0, W)], halo_send.at[2 * degree], halo_recv.at[2 * degree], row=up)
        )
        halo_down.append(
            remote(
                v.at[pl.ds(W, W)],
                v.at[pl.ds(rows_here + W, W)],
                halo_send.at[2 * degree + 1],
                halo_recv.at[2 * degree + 1],
                row=down,
            )
        )
    halo_up[0].start()
    halo_down[0].start()
    meta_copies = [
        remote(meta_out.at[k, pl.ds(0, 1)], meta_in.at[k, pl.ds(0, 1)], meta_send.at[k], meta_recv.at[k], col=at(k // SIDE, k % SIDE))
        for k in range(1, NB)
    ]
    meta_copies += [
        remote(core_out.at[pl.ds(0, SLOTS)], core_in.at[k, pl.ds(0, SLOTS)], core_send.at[k], core_recv.at[k], col=at(k // SIDE, k % SIDE))
        for k in range(1, NB)
    ]
    for copy in meta_copies:
        copy.start()

    part = 2 * KB // PIECES
    pieces = [(s, half, first) for s in range(CAP) for half in range(2) for first in range(0, KB, part)]

    def send_pieces(s, half, first):
        for dy, dz in OFFSETS:
            i = s * NB + dy * SIDE + dz
            remote(
                outgoing.at[i, half, pl.ds(first, part)],
                incoming.at[i, half, pl.ds(first, part)],
                basis_send.at[i],
                basis_recv.at[i],
                col=at(dy, dz),
            ).start()

    load_basis.wait()
    for s in range(CAP):
        incoming[s * NB] = basis_vm[owner[s * NB]]

        def pack(k, carry, s=s):
            outgoing[s * NB + k] = basis_vm[owner[s * NB + k]]
            return carry

        lax.fori_loop(1, NB, pack, 0)
        if s == 0:
            for piece in pieces[:EARLY]:
                send_pieces(*piece)

    for side, d in ((0, 1), (1, SIDE - 1)):
        for half, (dy, dz) in enumerate(((0, d), (d, 0))):
            band_wait(half, dy, dz)
            band_part(half, side).start()
    for d in (0, 1, SIDE - 1, 2):
        if d == 2:
            for half in range(2):
                band_part_wait(half, 0)
                band_part_wait(half, 1)
        for other in (1, SIDE - 1):
            band_copy(0, other, d).start()
            band_copy(1, d, other).start()
    for piece in pieces[EARLY : EARLY + 1]:
        send_pieces(*piece)
    for d in range(SIDE):
        near = 1 if d < 2 else SIDE - 1
        band_wait(0, near, d)
        band_copy(0, 2, d).start()
        band_wait(1, d, near)
        band_copy(1, d, 2).start()
    for piece in pieces[EARLY + 1 :]:
        send_pieces(*piece)

    for first in range(SIDE):
        for second in (2, SIDE - 1 if first < 2 else 1):
            band_wait(0, second, first)
            band_wait(1, first, second)

    row_at = lax.broadcasted_iota(jnp.int32, (W, W), 0)
    col_at = lax.broadcasted_iota(jnp.int32, (W, W), 1)

    def build(j, carry):
        coupling = bands[1, j].astype(jnp.float32)
        first = jnp.where((j == 0) & (r == 0), 0.0, 1.0)
        last = jnp.where((j == NB - 1) & (r == rows - 1), 0.0, 1.0)
        band[j, :, 0:W] = (jnp.where(col_at >= row_at, coupling, 0.0) * first).astype(jnp.bfloat16)
        band[j, :, W : 2 * W] = bands[0, j]
        band[j, :, 2 * W : 3 * W] = (jnp.where(col_at < row_at, coupling, 0.0) * last).astype(jnp.bfloat16)
        return carry

    lax.fori_loop(0, NB, build, 0)

    def apply(j, v):
        window = v[pl.ds(pl.multiple_of(j * W, W), 3 * W), :]
        return jnp.dot(band[j], window, preferred_element_type=jnp.float32)

    def inner(j):
        return pl.ds(pl.multiple_of((j + 1) * W, W), W)

    def degree_1(j, carry):
        value = apply(j, v0)
        total[j] = value
        v1[inner(j), :] = value.astype(jnp.bfloat16)
        return carry

    c0, c1, c2, c3 = (coef[i] for i in range(4))

    def degree_2(j, carry):
        start = v0[inner(j), :].astype(jnp.float32)
        value = 2.0 * apply(j, v1) - start
        v2[inner(j), :] = value.astype(jnp.bfloat16)
        total[j] = c0 * start + (c1 - c3) * total[j] + c2 * value
        return carry

    def degree_3(j, carry):
        value = total[j] + (2.0 * c3) * apply(j, v2)
        kern[j // 2, pl.ds(pl.multiple_of(lax.rem(j, 2) * W, W), W), :] = value.astype(jnp.bfloat16)
        return carry

    load_columns.wait()
    halo_up[0].wait()
    halo_down[0].wait()
    for step, degree in ((degree_1, 1), (degree_2, 2)):
        step(0, 0)
        step(NB - 1, 0)
        lax.fori_loop(1, NB // 2, step, 0)
        halo_up[degree].start()
        halo_down[degree].start()
        lax.fori_loop(NB // 2, NB - 1, step, 0)
        halo_up[degree].wait()
        halo_down[degree].wait()
    lax.fori_loop(0, NB, degree_3, 0)

    for copy in meta_copies:
        copy.wait()
    meta_copy = pltpu.make_async_copy(meta_in.at[:, pl.ds(0, 1)], meta_sm.at[:, pl.ds(0, 1)], local_sem.at[4])
    meta_copy.start()
    meta_copy.wait()
    for s in range(CAP):
        for k in range(NB):
            block_of[s * NB + k] = meta_sm[k, 0, ENTRIES + s]

    def basis_copy(i):
        return remote(outgoing.at[i], incoming.at[i], basis_send.at[i], basis_recv.at[i], col=at(0, 1))

    def project(s, k):
        i = s * NB + k
        keep = pltpu.make_async_copy(incoming.at[i], received.at[i], out_sem.at[i])
        keep.start()
        block = jnp.maximum(meta_sm[k, 0, ENTRIES + s], 0)
        product = jnp.dot(kern[block], incoming[i, 1], preferred_element_type=jnp.float32)
        return jnp.sum(product * incoming[i, 0].astype(jnp.float32), axis=0, keepdims=True) * (1.0 / KB)

    contrib_copies = []
    for s in range(CAP):
        contrib[c, s * NB : s * NB + 1, :] = project(s, 0)

        def step(k, carry, s=s):
            basis_copy(s * NB + k).wait_recv()
            contrib[c, pl.ds(s * NB + k, 1), :] = project(s, k)
            return carry

        lax.fori_loop(1, NB, step, 0)
        lines = contrib.at[c, pl.ds(s * NB, NB)]
        for k in range(1, NB):
            i = s * NB + k
            copy = remote(lines, lines, contrib_send.at[i], contrib_recv.at[i], col=at(k // SIDE, k % SIDE))
            copy.start()
            contrib_copies.append(copy)
    for s in range(CAP):
        for k in range(1, NB):
            i = s * NB + k
            lines = contrib.at[at(-(k // SIDE), -(k % SIDE)), pl.ds(s * NB, NB)]
            remote(lines, lines, contrib_send.at[i], contrib_recv.at[i], col=at(0, 1)).wait_recv()

    def density_of(k, tile):
        value = core_in[k, pl.ds(tile, 1), :]
        for slot in range(SLOTS):
            place = meta_sm[k, 0, tile * SLOTS + slot]
            there = jnp.maximum(place, 0)
            line = contrib[lax.div(there, CAP * NB), pl.ds(lax.rem(there, CAP * NB), 1), :]
            value = value + jnp.where(place >= 0, line, 0.0)
        return value

    for t in range(ENTRIES // SLOTS):
        dens[t : t + 1, :] = density_of(0, t)

    def slot_density(k, carry):
        for s in range(CAP):
            tile_density[pl.ds(s * NB + k, 1), :] = density_of(k, meta_sm[k, 0, ENTRIES + CAP + s])
        return carry

    lax.fori_loop(0, NB, slot_density, 0, unroll=True)
    x = jnp.maximum(tile_density[...], 0.1)
    root = jnp.exp(jnp.log(x) * (1.0 / 3.0))
    root = root - (root * root * root - x) / (3.0 * root * root)
    pot_in[...] = -exchange_factor * root

    for copy in contrib_copies:
        copy.wait_send()
    for half, skip in enumerate(((0, 2), (2, 0))):
        for dy, dz in OFFSETS:
            if (dy, dz) != skip:
                band_copy(half, dy, dz).wait_send()
        for side in range(2):
            band_part(half, side).wait_send()

    def finish(k, carry):
        for s in range(CAP):
            basis_copy(s * NB + k).wait_send()
        return carry

    lax.fori_loop(1, NB, finish, 0)

    def kept(i, carry):
        pltpu.make_async_copy(incoming.at[i], received.at[i], out_sem.at[i]).wait()
        return carry

    lax.fori_loop(0, CAP * NB, kept, 0)


def exchange(columns, ham, pattern, coef, peers, tile_block, tile_count, basis, core):
    any_spec = pl.BlockSpec(memory_space=pl.ANY)
    smem = pl.BlockSpec(memory_space=pltpu.SMEM)
    vmem = pl.BlockSpec(memory_space=pltpu.VMEM)
    rows_here = NB * W
    slots = CAP * NB
    bf16, f32, i32 = jnp.bfloat16, jnp.float32, jnp.int32
    dma = pltpu.SemaphoreType.DMA
    return pl.pallas_call(
        exchange_kernel,
        out_shape=(
            jax.ShapeDtypeStruct(core.shape, f32),
            jax.ShapeDtypeStruct((slots, 2, KB, P_SIZE), bf16),
            jax.ShapeDtypeStruct((slots, P_SIZE), f32),
            jax.ShapeDtypeStruct((slots,), i32),
        ),
        in_specs=[any_spec, any_spec, pl.BlockSpec(memory_space=pltpu.HBM), smem, smem, smem, smem, any_spec, vmem],
        out_specs=(vmem, any_spec, vmem, smem),
        scratch_shapes=[
            pltpu.SMEM((1,), i32),
            pltpu.VMEM((W, W), bf16),
            pltpu.VMEM((2, NB, W, W), bf16),
            pltpu.VMEM((NB, W, 3 * W), bf16),
            pltpu.VMEM((rows_here + 2 * W, KB), bf16),
            pltpu.VMEM((rows_here + 2 * W, KB), bf16),
            pltpu.VMEM((rows_here + 2 * W, KB), bf16),
            pltpu.VMEM((NB, W, KB), f32),
            pltpu.VMEM((rows_here // KB, KB, KB), bf16),
            pltpu.VMEM(basis.shape, bf16),
            pltpu.VMEM((slots, 2, KB, P_SIZE), bf16),
            pltpu.VMEM((slots, 2, KB, P_SIZE), bf16),
            pltpu.VMEM((NB, 8, P_SIZE), i32),
            pltpu.VMEM((NB, 8, P_SIZE), i32),
            pltpu.SMEM((NB, 8, P_SIZE), i32),
            pltpu.VMEM((8, P_SIZE), f32),
            pltpu.VMEM((NB, 8, P_SIZE), f32),
            pltpu.VMEM((NB, slots, P_SIZE), f32),
            pltpu.VMEM((slots, P_SIZE), f32),
            pltpu.SMEM((slots,), i32),
            dma((6,)),
            dma((slots,)),
            dma((2 * (NB - 1) + 4,)),
            dma((2 * (NB - 1) + 4,)),
            dma((NB,)),
            dma((NB,)),
            dma((6,)),
            dma((6,)),
            dma((slots,)),
            dma((slots,)),
            dma((slots,)),
            dma((slots,)),
            dma((NB,)),
            dma((NB,)),
        ],
        compiler_params=pltpu.CompilerParams(
            collective_id=0, has_side_effects=True, vmem_limit_bytes=66_000_000
        ),
        name="exchange",
    )(columns, ham, pattern, coef, peers, tile_block, tile_count, basis, core)


def update_kernel(
    received, pot, block_of, density, out, dens, pairs, lines, blocks, named, count, total, rounded, points, pair_sem, sem
):
    slots = CAP * NB
    row_blocks = NB * W // KB
    load_blocks = pltpu.make_async_copy(block_of, blocks, sem.at[0])
    load_lines = pltpu.make_async_copy(pot, lines, sem.at[1])
    load_blocks.start()
    load_lines.start()
    load_points = pltpu.make_async_copy(density, points, sem.at[2 + row_blocks])
    store_points = pltpu.make_async_copy(points, dens, sem.at[3 + row_blocks])
    load_points.start()
    for b in range(row_blocks):
        count[b] = 0
    load_blocks.wait()

    def load(i):
        return pltpu.make_async_copy(received.at[i], pairs.at[i], pair_sem.at[i])

    def sort(i, carry):
        block = blocks[i]

        @pl.when(block >= 0)
        def _():
            named[block * slots + count[block]] = i
            count[block] = count[block] + 1

        return carry

    lax.fori_loop(0, slots, sort, 0)

    def fetch(b, carry):
        def one(j, carry):
            load(named[b * slots + j]).start()
            return carry

        return lax.fori_loop(0, count[b], one, carry)

    lax.fori_loop(0, row_blocks, fetch, 0)
    load_lines.wait()
    load_points.wait()
    store_points.start()

    def store(b):
        return pltpu.make_async_copy(rounded.at[b], out.at[b], sem.at[2 + b])

    def weighted(i, present):
        line = jnp.where(present, lines[pl.ds(i, 1), :], 0.0)
        return (pairs[i, 1].astype(jnp.float32) * line).astype(jnp.bfloat16)

    def product(b, j, n):
        first = named[b * slots + 2 * j]
        paired = 2 * j + 1 < n
        second = jnp.where(paired, named[b * slots + 2 * j + 1], first)
        load(first).wait()

        @pl.when(paired)
        def _():
            load(second).wait()

        left = jnp.concatenate([pairs[first, 0], pairs[second, 0]], axis=1)
        right = jnp.concatenate([weighted(first, True), weighted(second, paired)], axis=1)
        return lax.dot_general(left, right, (((1,), (1,)), ((), ())), preferred_element_type=jnp.float32)

    def block_sum(b, carry):
        n = count[b]
        last = lax.div(n + 1, 2) - 1

        def add(j, carry):
            total[...] = jnp.where(j > 0, total[...], 0.0) + product(b, j, n)
            return carry

        lax.fori_loop(0, last, add, 0)

        @pl.when(n > 0)
        def _():
            value = jnp.where(last > 0, total[...], 0.0) + product(b, last, n)
            rounded[b] = (value * (1.0 / math.sqrt(P_SIZE))).astype(jnp.bfloat16)

        @pl.when(n == 0)
        def _():
            rounded[b] = jnp.zeros((KB, KB), jnp.bfloat16)

        store(b).start()
        return carry

    lax.fori_loop(0, row_blocks, block_sum, 0)
    for b in range(row_blocks):
        store(b).wait()
    store_points.wait()


def update(block_of, received, pot_in, density):
    blocks = NB * W // KB
    any_spec = pl.BlockSpec(memory_space=pl.ANY)
    return pl.pallas_call(
        update_kernel,
        out_shape=(
            jax.ShapeDtypeStruct((blocks, KB, KB), jnp.bfloat16),
            jax.ShapeDtypeStruct(density.shape, density.dtype),
        ),
        in_specs=[any_spec] * 4,
        out_specs=(any_spec, any_spec),
        scratch_shapes=[
            pltpu.VMEM(received.shape, received.dtype),
            pltpu.VMEM(pot_in.shape, pot_in.dtype),
            pltpu.SMEM(block_of.shape, block_of.dtype),
            pltpu.SMEM((blocks * CAP * NB,), jnp.int32),
            pltpu.SMEM((blocks,), jnp.int32),
            pltpu.VMEM((KB, KB), jnp.float32),
            pltpu.VMEM((blocks, KB, KB), jnp.bfloat16),
            pltpu.VMEM(density.shape, density.dtype),
            pltpu.SemaphoreType.DMA((CAP * NB,)),
            pltpu.SemaphoreType.DMA((4 + blocks,)),
        ],
        compiler_params=pltpu.CompilerParams(vmem_limit_bytes=67_000_000),
        name="update",
    )(received, pot_in, block_of, density)


def shards(columns, ham, pattern, coef, peers, tile_block, tile_count, basis, core):
    dens, received, pot_in, block_of = exchange(
        columns, ham, pattern, coef, peers.reshape(-1), tile_block, tile_count, basis, core
    )
    blocks, dens = update(block_of, received, pot_in, dens)
    return dens, blocks.reshape(columns.shape)


def solution(mesh):
    return jax.shard_map(
        shards,
        mesh=mesh,
        in_specs=(
            P("row", "col"),
            P(("row", "col"), None, None, None),
            P(("row", "col")),
            P(),
            P(("row", "col"), None),
            P(("row", "col")),
            P(("row", "col")),
            P(("row", "col"), None, None, None),
            P(("row", "col"), None),
        ),
        out_specs=(P(("row", "col"), None), P("row", "col")),
        check_vma=False,
    )
```

```python
import functools
import math

import jax
import jax.numpy as jnp
from jax import lax
from jax.experimental import pallas as pl
from jax.experimental.pallas import tpu as pltpu
from jax.sharding import PartitionSpec as P

MESH = pl.DeviceIdType.MESH
W = 256
KB = 512
SLOTS = 4
CAP = 2
P_SIZE = 128
GROUP = 4
NB = 16
ENTRIES = 16
PIECES = 8
EARLY = 1
SIDE = 4
OFFSETS = tuple((k // SIDE, k % SIDE) for k in range(1, NB))

exchange_factor = (3.0 / math.pi) ** (1.0 / 3.0)


def exchange_kernel(
    columns,
    ham,
    pattern,
    coef_at,
    peers_at,
    block_at,
    count_at,
    basis,
    core_at,
    dens,
    received,
    pot_in,
    block_of,
    present,
    coef,
    peers,
    tile_block,
    tile_count,
    core,
    own_ham,
    bands,
    band,
    v0,
    v1,
    v2,
    total,
    kern,
    basis_vm,
    outgoing,
    incoming,
    meta_out,
    meta_in,
    meta_sm,
    core_out,
    core_in,
    contrib,
    tile_density,
    owner,
    local_sem,
    out_sem,
    band_send,
    band_recv,
    meta_send,
    meta_recv,
    halo_send,
    halo_recv,
    basis_send,
    basis_recv,
    contrib_send,
    contrib_recv,
    core_send,
    core_recv,
):
    r = lax.axis_index("row")
    c = lax.axis_index("col")
    rows = lax.axis_size("row")
    y, z = c // SIDE, c % SIDE
    rows_here = NB * W

    def at(dy, dz):
        return lax.rem(y + dy + SIDE, SIDE) * SIDE + lax.rem(z + dz + SIDE, SIDE)

    def remote(src, dst, send, recv, **where):
        return pltpu.make_async_remote_copy(
            src_ref=src, dst_ref=dst, send_sem=send, recv_sem=recv, device_id=where, device_id_type=MESH
        )

    up, down = lax.rem(r + 1, rows), lax.rem(r + rows - 1, rows)

    barrier = pltpu.get_barrier_semaphore()
    for dy, dz in OFFSETS:
        pl.semaphore_signal(barrier, inc=1, device_id={"col": at(dy, dz)}, device_id_type=MESH)
    for row in (up, down):
        pl.semaphore_signal(barrier, inc=1, device_id={"row": row}, device_id_type=MESH)

    load_diag = pltpu.make_async_copy(ham.at[0, 0], bands.at[0, c], local_sem.at[0])
    load_coupling = pltpu.make_async_copy(ham.at[0, 1], own_ham, local_sem.at[1])
    load_basis = pltpu.make_async_copy(basis, basis_vm, local_sem.at[2])
    load_columns = pltpu.make_async_copy(columns, v0.at[pl.ds(W, rows_here)], local_sem.at[3])
    small = [
        pltpu.make_async_copy(source, target, local_sem.at[5 + i])
        for i, (source, target) in enumerate(
            (
                (peers_at, peers),
                (count_at, tile_count),
                (block_at, tile_block),
                (core_at, core),
                (coef_at, coef),
                (pattern, present),
            )
        )
    ]
    for copy in small:
        copy.start()
    load_diag.start()
    load_coupling.start()
    load_basis.start()
    load_columns.start()

    for copy in small:
        copy.wait()
    core_out[...] = jnp.concatenate([core[...], jnp.zeros_like(core[...])], axis=0)
    core_in[0] = core_out[...]
    lane = lax.broadcasted_iota(jnp.int32, (8, P_SIZE), 1)
    codes = jnp.full((8, P_SIZE), -1, jnp.int32)
    slots_of = []
    for k in range(NB):
        peer = at(k // SIDE, k % SIDE)
        first, second = jnp.int32(ENTRIES), jnp.int32(ENTRIES)
        for e in reversed(range(ENTRIES)):
            named = peers[e] == peer
            second = jnp.where(named, first, second)
            first = jnp.where(named, jnp.int32(e), first)
        fields = []
        for s, found in enumerate((first, second)):
            entry = jnp.minimum(found, ENTRIES - 1)
            live = (found < ENTRIES) & (lax.rem(entry, SLOTS) < tile_count[lax.div(entry, SLOTS)])
            owner[s * NB + k] = entry
            fields.append((jnp.where(live, tile_block[entry], -1), lax.div(entry, SLOTS)))
            codes = jnp.where((lane == entry) & live, peer * (CAP * NB) + s * NB + k, codes)
        slots_of.append(fields)
    for k in range(NB):
        words = codes
        for s in range(CAP):
            words = jnp.where(lane == ENTRIES + s, slots_of[k][s][0], words)
            words = jnp.where(lane == ENTRIES + CAP + s, slots_of[k][s][1], words)
        if k == 0:
            meta_in[0] = words
        else:
            meta_out[k] = words

    load_coupling.wait()
    bands[1, c] = (own_ham[...].astype(jnp.float32) * present[0].astype(jnp.float32)).astype(jnp.bfloat16)
    load_diag.wait()
    pl.semaphore_wait(barrier, NB - 1 + 2)

    def band_copy(half, dy, dz):
        first, second = (dz, dy) if half == 0 else (dy, dz)
        done, hop = (first, second) if second else (0, first)
        before = 0
        if second == 2:
            hop, before = (1, 1) if first < 2 else (-1, -1)
        if half == 0:
            source, there = at(-before, -done), (at(hop, 0) if second else at(0, hop))
        else:
            source, there = at(-done, -before), (at(0, hop) if second else at(hop, 0))
        i = half * (NB - 1) + dy * SIDE + dz - 1
        return remote(bands.at[half, source], bands.at[half, source], band_send.at[i], band_recv.at[i], col=there)

    def band_wait(half, dy, dz):
        i = half * (NB - 1) + dy * SIDE + dz - 1
        block = bands.at[half, at(-dy, -dz)]
        remote(block, block, band_send.at[i], band_recv.at[i], col=at(dy, dz)).wait_recv()

    def band_part(half, side):
        hop = 1 - 2 * side
        along = (lambda step: at(0, step)) if half == 0 else (lambda step: at(step, 0))
        part = bands.at[half, along(-hop), pl.ds(side * (W // 2), W // 2)]
        i = 2 * (NB - 1) + 2 * half + side
        return remote(part, part, band_send.at[i], band_recv.at[i], col=along(hop))

    def band_part_wait(half, side):
        along = (lambda step: at(0, step)) if half == 0 else (lambda step: at(step, 0))
        part = bands.at[half, along(2), pl.ds(side * (W // 2), W // 2)]
        i = 2 * (NB - 1) + 2 * half + side
        remote(part, part, band_send.at[i], band_recv.at[i], col=along(1)).wait_recv()

    for d in (1, SIDE - 1):
        band_copy(0, 0, d).start()
        band_copy(1, d, 0).start()
    halo_up = [remote(columns.at[pl.ds(rows_here - W, W)], v0.at[pl.ds(0, W)], halo_send.at[0], halo_recv.at[0], row=up)]
    halo_down = [remote(columns.at[pl.ds(0, W)], v0.at[pl.ds(rows_here + W, W)], halo_send.at[1], halo_recv.at[1], row=down)]
    for degree, v in ((1, v1), (2, v2)):
        halo_up.append(
            remote(v.at[pl.ds(rows_here, W)], v.at[pl.ds(0, W)], halo_send.at[2 * degree], halo_recv.at[2 * degree], row=up)
        )
        halo_down.append(
            remote(
                v.at[pl.ds(W, W)],
                v.at[pl.ds(rows_here + W, W)],
                halo_send.at[2 * degree + 1],
                halo_recv.at[2 * degree + 1],
                row=down,
            )
        )
    halo_up[0].start()
    halo_down[0].start()
    meta_copies = [
        remote(meta_out.at[k, pl.ds(0, 1)], meta_in.at[k, pl.ds(0, 1)], meta_send.at[k], meta_recv.at[k], col=at(k // SIDE, k % SIDE))
        for k in range(1, NB)
    ]
    meta_copies += [
        remote(core_out.at[pl.ds(0, SLOTS)], core_in.at[k, pl.ds(0, SLOTS)], core_send.at[k], core_recv.at[k], col=at(k // SIDE, k % SIDE))
        for k in range(1, NB)
    ]
    for copy in meta_copies:
        copy.start()

    part = 2 * KB // PIECES
    pieces = [(s, half, first) for s in range(CAP) for half in range(2) for first in range(0, KB, part)]

    def send_pieces(s, half, first):
        for dy, dz in OFFSETS:
            i = s * NB + dy * SIDE + dz
            remote(
                outgoing.at[i, half, pl.ds(first, part)],
                incoming.at[i, half, pl.ds(first, part)],
                basis_send.at[i],
                basis_recv.at[i],
                col=at(dy, dz),
            ).start()

    load_basis.wait()
    for s in range(CAP):
        incoming[s * NB] = basis_vm[owner[s * NB]]

        def pack(k, carry, s=s):
            outgoing[s * NB + k] = basis_vm[owner[s * NB + k]]
            return carry

        lax.fori_loop(1, NB, pack, 0)
        if s == 0:
            for piece in pieces[:EARLY]:
                send_pieces(*piece)

    for side, d in ((0, 1), (1, SIDE - 1)):
        for half, (dy, dz) in enumerate(((0, d), (d, 0))):
            band_wait(half, dy, dz)
            band_part(half, side).start()
    for d in (0, 1, SIDE - 1, 2):
        if d == 2:
            for half in range(2):
                band_part_wait(half, 0)
                band_part_wait(half, 1)
        for other in (1, SIDE - 1):
            band_copy(0, other, d).start()
            band_copy(1, d, other).start()
    for piece in pieces[EARLY : EARLY + 1]:
        send_pieces(*piece)
    for d in range(SIDE):
        near = 1 if d < 2 else SIDE - 1
        band_wait(0, near, d)
        band_copy(0, 2, d).start()
        band_wait(1, d, near)
        band_copy(1, d, 2).start()
    for piece in pieces[EARLY + 1 :]:
        send_pieces(*piece)

    for first in range(SIDE):
        for second in (2, SIDE - 1 if first < 2 else 1):
            band_wait(0, second, first)
            band_wait(1, first, second)

    row_at = lax.broadcasted_iota(jnp.int32, (W, W), 0)
    col_at = lax.broadcasted_iota(jnp.int32, (W, W), 1)

    def build(j, carry):
        coupling = bands[1, j].astype(jnp.float32)
        first = jnp.where((j == 0) & (r == 0), 0.0, 1.0)
        last = jnp.where((j == NB - 1) & (r == rows - 1), 0.0, 1.0)
        band[j, :, 0:W] = (jnp.where(col_at >= row_at, coupling, 0.0) * first).astype(jnp.bfloat16)
        band[j, :, W : 2 * W] = bands[0, j]
        band[j, :, 2 * W : 3 * W] = (jnp.where(col_at < row_at, coupling, 0.0) * last).astype(jnp.bfloat16)
        return carry

    lax.fori_loop(0, NB, build, 0)

    def apply(j, v):
        window = v[pl.ds(pl.multiple_of(j * W, W), 3 * W), :]
        return jnp.dot(band[j], window, preferred_element_type=jnp.float32)

    def inner(j):
        return pl.ds(pl.multiple_of((j + 1) * W, W), W)

    def degree_1(j, carry):
        value = apply(j, v0)
        total[j] = value
        v1[inner(j), :] = value.astype(jnp.bfloat16)
        return carry

    c0, c1, c2, c3 = (coef[i] for i in range(4))

    def degree_2(j, carry):
        start = v0[inner(j), :].astype(jnp.float32)
        value = 2.0 * apply(j, v1) - start
        v2[inner(j), :] = value.astype(jnp.bfloat16)
        total[j] = c0 * start + (c1 - c3) * total[j] + c2 * value
        return carry

    def degree_3(j, carry):
        value = total[j] + (2.0 * c3) * apply(j, v2)
        kern[j // 2, pl.ds(pl.multiple_of(lax.rem(j, 2) * W, W), W), :] = value.astype(jnp.bfloat16)
        return carry

    load_columns.wait()
    halo_up[0].wait()
    halo_down[0].wait()
    for step, degree in ((degree_1, 1), (degree_2, 2)):
        step(0, 0)
        step(NB - 1, 0)
        lax.fori_loop(1, NB // 2, step, 0)
        halo_up[degree].start()
        halo_down[degree].start()
        lax.fori_loop(NB // 2, NB - 1, step, 0)
        halo_up[degree].wait()
        halo_down[degree].wait()
    lax.fori_loop(0, NB, degree_3, 0)

    for copy in meta_copies:
        copy.wait()
    meta_copy = pltpu.make_async_copy(meta_in.at[:, pl.ds(0, 1)], meta_sm.at[:, pl.ds(0, 1)], local_sem.at[4])
    meta_copy.start()
    meta_copy.wait()
    for s in range(CAP):
        for k in range(NB):
            block_of[s * NB + k] = meta_sm[k, 0, ENTRIES + s]

    def basis_copy(i):
        return remote(outgoing.at[i], incoming.at[i], basis_send.at[i], basis_recv.at[i], col=at(0, 1))

    def project(s, k):
        i = s * NB + k
        keep = pltpu.make_async_copy(incoming.at[i], received.at[i], out_sem.at[i])
        keep.start()
        block = jnp.maximum(meta_sm[k, 0, ENTRIES + s], 0)
        product = jnp.dot(kern[block], incoming[i, 1], preferred_element_type=jnp.float32)
        return jnp.sum(product * incoming[i, 0].astype(jnp.float32), axis=0, keepdims=True) * (1.0 / KB)

    contrib_copies = []
    groups = ((0, 0, NB), (1, 0, NB // 2), (1, NB // 2, NB))
    for g, (s, begin, end) in enumerate(groups):
        if begin == 0:
            contrib[c, s * NB : s * NB + 1, :] = project(s, 0)

        def step(k, carry, s=s):
            basis_copy(s * NB + k).wait_recv()
            contrib[c, pl.ds(s * NB + k, 1), :] = project(s, k)
            return carry

        lax.fori_loop(max(begin, 1), end, step, 0)
        rows_of = pl.ds(s * NB + begin, end - begin)
        lines = contrib.at[c, rows_of]
        for k in range(1, NB):
            i = g * NB + k
            copy = remote(lines, lines, contrib_send.at[i], contrib_recv.at[i], col=at(k // SIDE, k % SIDE))
            copy.start()
            contrib_copies.append(copy)
    for g, (s, begin, end) in enumerate(groups):
        for k in range(1, NB):
            i = g * NB + k
            lines = contrib.at[at(-(k // SIDE), -(k % SIDE)), pl.ds(s * NB + begin, end - begin)]
            remote(lines, lines, contrib_send.at[i], contrib_recv.at[i], col=at(0, 1)).wait_recv()

    def density_of(k, tile):
        value = core_in[k, pl.ds(tile, 1), :]
        for slot in range(SLOTS):
            place = meta_sm[k, 0, tile * SLOTS + slot]
            there = jnp.maximum(place, 0)
            line = contrib[lax.div(there, CAP * NB), pl.ds(lax.rem(there, CAP * NB), 1), :]
            value = value + jnp.where(place >= 0, line, 0.0)
        return value

    for t in range(ENTRIES // SLOTS):
        dens[t : t + 1, :] = density_of(0, t)

    def slot_density(k, carry):
        for s in range(CAP):
            tile_density[pl.ds(s * NB + k, 1), :] = density_of(k, meta_sm[k, 0, ENTRIES + CAP + s])
        return carry

    lax.fori_loop(0, NB, slot_density, 0, unroll=True)
    x = jnp.maximum(tile_density[...], 0.1)
    root = jnp.exp(jnp.log(x) * (1.0 / 3.0))
    root = root - (root * root * root - x) / (3.0 * root * root)
    pot_in[...] = -exchange_factor * root

    for copy in contrib_copies:
        copy.wait_send()
    for half, skip in enumerate(((0, 2), (2, 0))):
        for dy, dz in OFFSETS:
            if (dy, dz) != skip:
                band_copy(half, dy, dz).wait_send()
        for side in range(2):
            band_part(half, side).wait_send()

    def finish(k, carry):
        for s in range(CAP):
            basis_copy(s * NB + k).wait_send()
        return carry

    lax.fori_loop(1, NB, finish, 0)

    def kept(i, carry):
        pltpu.make_async_copy(incoming.at[i], received.at[i], out_sem.at[i]).wait()
        return carry

    lax.fori_loop(0, CAP * NB, kept, 0)


def exchange(columns, ham, pattern, coef, peers, tile_block, tile_count, basis, core):
    any_spec = pl.BlockSpec(memory_space=pl.ANY)
    smem = pl.BlockSpec(memory_space=pltpu.SMEM)
    vmem = pl.BlockSpec(memory_space=pltpu.VMEM)
    rows_here = NB * W
    slots = CAP * NB
    bf16, f32, i32 = jnp.bfloat16, jnp.float32, jnp.int32
    dma = pltpu.SemaphoreType.DMA
    return pl.pallas_call(
        exchange_kernel,
        out_shape=(
            jax.ShapeDtypeStruct(core.shape, f32),
            jax.ShapeDtypeStruct((slots, 2, KB, P_SIZE), bf16),
            jax.ShapeDtypeStruct((slots, P_SIZE), f32),
            jax.ShapeDtypeStruct((slots,), i32),
        ),
        in_specs=[any_spec] * 9,
        out_specs=(vmem, any_spec, vmem, smem),
        scratch_shapes=[
            pltpu.SMEM((1,), i32),
            pltpu.SMEM(coef.shape, f32),
            pltpu.SMEM(peers.shape, i32),
            pltpu.SMEM(tile_block.shape, i32),
            pltpu.SMEM(tile_count.shape, i32),
            pltpu.VMEM(core.shape, f32),
            pltpu.VMEM((W, W), bf16),
            pltpu.VMEM((2, NB, W, W), bf16),
            pltpu.VMEM((NB, W, 3 * W), bf16),
            pltpu.VMEM((rows_here + 2 * W, KB), bf16),
            pltpu.VMEM((rows_here + 2 * W, KB), bf16),
            pltpu.VMEM((rows_here + 2 * W, KB), bf16),
            pltpu.VMEM((NB, W, KB), f32),
            pltpu.VMEM((rows_here // KB, KB, KB), bf16),
            pltpu.VMEM(basis.shape, bf16),
            pltpu.VMEM((slots, 2, KB, P_SIZE), bf16),
            pltpu.VMEM((slots, 2, KB, P_SIZE), bf16),
            pltpu.VMEM((NB, 8, P_SIZE), i32),
            pltpu.VMEM((NB, 8, P_SIZE), i32),
            pltpu.SMEM((NB, 8, P_SIZE), i32),
            pltpu.VMEM((8, P_SIZE), f32),
            pltpu.VMEM((NB, 8, P_SIZE), f32),
            pltpu.VMEM((NB, slots, P_SIZE), f32),
            pltpu.VMEM((slots, P_SIZE), f32),
            pltpu.SMEM((slots,), i32),
            dma((11,)),
            dma((slots,)),
            dma((2 * (NB - 1) + 4,)),
            dma((2 * (NB - 1) + 4,)),
            dma((NB,)),
            dma((NB,)),
            dma((6,)),
            dma((6,)),
            dma((slots,)),
            dma((slots,)),
            dma((3 * NB,)),
            dma((3 * NB,)),
            dma((NB,)),
            dma((NB,)),
        ],
        compiler_params=pltpu.CompilerParams(
            collective_id=0, has_side_effects=True, vmem_limit_bytes=66_000_000
        ),
        name="exchange",
    )(columns, ham, pattern, coef, peers, tile_block, tile_count, basis, core)


def update_kernel(
    received, pot, block_of, density, out, dens, pairs, lines, blocks, named, count, total, rounded, points, pair_sem, sem
):
    slots = CAP * NB
    row_blocks = NB * W // KB
    load_blocks = pltpu.make_async_copy(block_of, blocks, sem.at[0])
    load_lines = pltpu.make_async_copy(pot, lines, sem.at[1])
    load_blocks.start()
    load_lines.start()
    load_points = pltpu.make_async_copy(density, points, sem.at[2 + row_blocks])
    store_points = pltpu.make_async_copy(points, dens, sem.at[3 + row_blocks])
    load_points.start()
    for b in range(row_blocks):
        count[b] = 0
    load_blocks.wait()

    def load(i):
        return pltpu.make_async_copy(received.at[i], pairs.at[i], pair_sem.at[i])

    def sort(i, carry):
        block = blocks[i]

        @pl.when(block >= 0)
        def _():
            named[block * slots + count[block]] = i
            count[block] = count[block] + 1

        return carry

    lax.fori_loop(0, slots, sort, 0)

    def fetch(b, carry):
        def one(j, carry):
            load(named[b * slots + j]).start()
            return carry

        return lax.fori_loop(0, count[b], one, carry)

    lax.fori_loop(0, row_blocks, fetch, 0)
    load_lines.wait()
    load_points.wait()
    store_points.start()

    def store(b):
        return pltpu.make_async_copy(rounded.at[b], out.at[b], sem.at[2 + b])

    def weighted(i, present):
        line = jnp.where(present, lines[pl.ds(i, 1), :], 0.0)
        return (pairs[i, 1].astype(jnp.float32) * line).astype(jnp.bfloat16)

    def product(b, j, n, group):
        first = named[b * slots + group * j]
        left, right = [], []
        for q in range(group):
            here = group * j + q < n
            i = jnp.where(here, named[b * slots + group * j + q], first)

            @pl.when(here)
            def _(i=i):
                load(i).wait()

            left.append(i)
            right.append(here)
        return lax.dot_general(
            jnp.concatenate([pairs[i, 0] for i in left], axis=1),
            jnp.concatenate([weighted(i, here) for i, here in zip(left, right)], axis=1),
            (((1,), (1,)), ((), ())),
            preferred_element_type=jnp.float32,
        )

    scale = 1.0 / math.sqrt(P_SIZE)

    def block_sum(b, carry):
        n = count[b]

        @pl.when(n == 0)
        def _():
            rounded[b] = jnp.zeros((KB, KB), jnp.bfloat16)

        for fewer, group in ((0, 2), (2, GROUP)):

            @pl.when((n > fewer) & (n <= group))
            def _(group=group):
                rounded[b] = (product(b, 0, n, group) * scale).astype(jnp.bfloat16)

        @pl.when(n > GROUP)
        def _():
            total[...] = jnp.zeros_like(total)

            def add(j, carry):
                total[...] = total[...] + product(b, j, n, GROUP)
                return carry

            lax.fori_loop(0, lax.div(n + GROUP - 1, GROUP), add, 0)
            rounded[b] = (total[...] * scale).astype(jnp.bfloat16)

        store(b).start()
        return carry

    lax.fori_loop(0, row_blocks, block_sum, 0)
    for b in range(row_blocks):
        store(b).wait()
    store_points.wait()


def update(block_of, received, pot_in, density):
    blocks = NB * W // KB
    any_spec = pl.BlockSpec(memory_space=pl.ANY)
    return pl.pallas_call(
        update_kernel,
        out_shape=(
            jax.ShapeDtypeStruct((blocks, KB, KB), jnp.bfloat16),
            jax.ShapeDtypeStruct(density.shape, density.dtype),
        ),
        in_specs=[any_spec] * 4,
        out_specs=(any_spec, any_spec),
        scratch_shapes=[
            pltpu.VMEM(received.shape, received.dtype),
            pltpu.VMEM(pot_in.shape, pot_in.dtype),
            pltpu.SMEM(block_of.shape, block_of.dtype),
            pltpu.SMEM((blocks * CAP * NB,), jnp.int32),
            pltpu.SMEM((blocks,), jnp.int32),
            pltpu.VMEM((KB, KB), jnp.float32),
            pltpu.VMEM((blocks, KB, KB), jnp.bfloat16),
            pltpu.VMEM(density.shape, density.dtype),
            pltpu.SemaphoreType.DMA((CAP * NB,)),
            pltpu.SemaphoreType.DMA((4 + blocks,)),
        ],
        compiler_params=pltpu.CompilerParams(vmem_limit_bytes=67_000_000),
        name="update",
    )(received, pot_in, block_of, density)


def shards(columns, ham, pattern, coef, peers, tile_block, tile_count, basis, core):
    dens, received, pot_in, block_of = exchange(
        columns, ham, pattern, coef, peers.reshape(-1), tile_block, tile_count, basis, core
    )
    blocks, dens = update(block_of, received, pot_in, dens)
    return dens, blocks.reshape(columns.shape)


def solution(mesh):
    return jax.shard_map(
        shards,
        mesh=mesh,
        in_specs=(
            P("row", "col"),
            P(("row", "col"), None, None, None),
            P(("row", "col")),
            P(),
            P(("row", "col"), None),
            P(("row", "col")),
            P(("row", "col")),
            P(("row", "col"), None, None, None),
            P(("row", "col"), None),
        ),
        out_specs=(P(("row", "col"), None), P("row", "col")),
        check_vma=False,
    )
```

```python
import functools
import math

import jax
import jax.numpy as jnp
from jax import lax
from jax.experimental import pallas as pl
from jax.experimental.pallas import tpu as pltpu
from jax.sharding import PartitionSpec as P

MESH = pl.DeviceIdType.MESH
W = 256
KB = 512
SLOTS = 4
CAP = 2
P_SIZE = 128
GROUP = 4
NB = 16
ENTRIES = 16
PIECES = 8
EARLY = 1
SIDE = 4
OFFSETS = tuple((k // SIDE, k % SIDE) for k in range(1, NB))


def hops(offset):
    return sum(min(d, SIDE - d) for d in offset)


OFF = ((0, 0),) + tuple(sorted(OFFSETS, key=hops, reverse=True))

exchange_factor = (3.0 / math.pi) ** (1.0 / 3.0)


def exchange_kernel(
    columns,
    ham,
    pattern,
    coef_at,
    peers_at,
    block_at,
    count_at,
    basis,
    core_at,
    dens,
    received,
    pot_in,
    block_of,
    present,
    coef,
    peers,
    tile_block,
    tile_count,
    core,
    own_ham,
    bands,
    band,
    v0,
    v1,
    v2,
    total,
    kern,
    basis_vm,
    outgoing,
    incoming,
    meta_out,
    meta_in,
    meta_sm,
    core_out,
    core_in,
    contrib,
    tile_density,
    owner,
    local_sem,
    out_sem,
    band_send,
    band_recv,
    meta_send,
    meta_recv,
    halo_send,
    halo_recv,
    basis_send,
    basis_recv,
    contrib_send,
    contrib_recv,
    core_send,
    core_recv,
):
    r = lax.axis_index("row")
    c = lax.axis_index("col")
    rows = lax.axis_size("row")
    y, z = c // SIDE, c % SIDE
    rows_here = NB * W

    def at(dy, dz):
        return lax.rem(y + dy + SIDE, SIDE) * SIDE + lax.rem(z + dz + SIDE, SIDE)

    def remote(src, dst, send, recv, **where):
        return pltpu.make_async_remote_copy(
            src_ref=src, dst_ref=dst, send_sem=send, recv_sem=recv, device_id=where, device_id_type=MESH
        )

    up, down = lax.rem(r + 1, rows), lax.rem(r + rows - 1, rows)

    barrier = pltpu.get_barrier_semaphore()
    for dy, dz in OFFSETS:
        pl.semaphore_signal(barrier, inc=1, device_id={"col": at(dy, dz)}, device_id_type=MESH)
    for row in (up, down):
        pl.semaphore_signal(barrier, inc=1, device_id={"row": row}, device_id_type=MESH)

    load_diag = pltpu.make_async_copy(ham.at[0, 0], bands.at[0, c], local_sem.at[0])
    load_coupling = pltpu.make_async_copy(ham.at[0, 1], own_ham, local_sem.at[1])
    load_basis = pltpu.make_async_copy(basis, basis_vm, local_sem.at[2])
    load_columns = pltpu.make_async_copy(columns, v0.at[pl.ds(W, rows_here)], local_sem.at[3])
    small = [
        pltpu.make_async_copy(source, target, local_sem.at[5 + i])
        for i, (source, target) in enumerate(
            (
                (peers_at, peers),
                (count_at, tile_count),
                (block_at, tile_block),
                (core_at, core),
                (coef_at, coef),
                (pattern, present),
            )
        )
    ]
    for copy in small:
        copy.start()
    load_diag.start()
    load_coupling.start()
    load_basis.start()
    load_columns.start()

    for copy in small:
        copy.wait()
    core_out[...] = jnp.concatenate([core[...], jnp.zeros_like(core[...])], axis=0)
    core_in[0] = core_out[...]
    lane = lax.broadcasted_iota(jnp.int32, (8, P_SIZE), 1)
    codes = jnp.full((8, P_SIZE), -1, jnp.int32)
    slots_of = []
    for k in range(NB):
        peer = at(*OFF[k])
        first, second = jnp.int32(ENTRIES), jnp.int32(ENTRIES)
        for e in reversed(range(ENTRIES)):
            named = peers[e] == peer
            second = jnp.where(named, first, second)
            first = jnp.where(named, jnp.int32(e), first)
        fields = []
        for s, found in enumerate((first, second)):
            entry = jnp.minimum(found, ENTRIES - 1)
            live = (found < ENTRIES) & (lax.rem(entry, SLOTS) < tile_count[lax.div(entry, SLOTS)])
            owner[s * NB + k] = entry
            fields.append((jnp.where(live, tile_block[entry], -1), lax.div(entry, SLOTS)))
            codes = jnp.where((lane == entry) & live, peer * (CAP * NB) + s * NB + k, codes)
        slots_of.append(fields)
    for k in range(NB):
        words = codes
        for s in range(CAP):
            words = jnp.where(lane == ENTRIES + s, slots_of[k][s][0], words)
            words = jnp.where(lane == ENTRIES + CAP + s, slots_of[k][s][1], words)
        if k == 0:
            meta_in[0] = words
        else:
            meta_out[k] = words

    load_coupling.wait()
    bands[1, c] = (own_ham[...].astype(jnp.float32) * present[0].astype(jnp.float32)).astype(jnp.bfloat16)
    load_diag.wait()
    pl.semaphore_wait(barrier, NB - 1 + 2)

    def band_copy(half, dy, dz):
        first, second = (dz, dy) if half == 0 else (dy, dz)
        done, hop = (first, second) if second else (0, first)
        before = 0
        if second == 2:
            hop, before = (1, 1) if first < 2 else (-1, -1)
        if half == 0:
            source, there = at(-before, -done), (at(hop, 0) if second else at(0, hop))
        else:
            source, there = at(-done, -before), (at(0, hop) if second else at(hop, 0))
        i = half * (NB - 1) + dy * SIDE + dz - 1
        return remote(bands.at[half, source], bands.at[half, source], band_send.at[i], band_recv.at[i], col=there)

    def band_wait(half, dy, dz):
        i = half * (NB - 1) + dy * SIDE + dz - 1
        block = bands.at[half, at(-dy, -dz)]
        remote(block, block, band_send.at[i], band_recv.at[i], col=at(dy, dz)).wait_recv()

    def band_part(half, side):
        hop = 1 - 2 * side
        along = (lambda step: at(0, step)) if half == 0 else (lambda step: at(step, 0))
        part = bands.at[half, along(-hop), pl.ds(side * (W // 2), W // 2)]
        i = 2 * (NB - 1) + 2 * half + side
        return remote(part, part, band_send.at[i], band_recv.at[i], col=along(hop))

    def band_part_wait(half, side):
        along = (lambda step: at(0, step)) if half == 0 else (lambda step: at(step, 0))
        part = bands.at[half, along(2), pl.ds(side * (W // 2), W // 2)]
        i = 2 * (NB - 1) + 2 * half + side
        remote(part, part, band_send.at[i], band_recv.at[i], col=along(1)).wait_recv()

    for d in (1, SIDE - 1):
        band_copy(0, 0, d).start()
        band_copy(1, d, 0).start()
    halo_up = [remote(columns.at[pl.ds(rows_here - W, W)], v0.at[pl.ds(0, W)], halo_send.at[0], halo_recv.at[0], row=up)]
    halo_down = [remote(columns.at[pl.ds(0, W)], v0.at[pl.ds(rows_here + W, W)], halo_send.at[1], halo_recv.at[1], row=down)]
    for degree, v in ((1, v1), (2, v2)):
        halo_up.append(
            remote(v.at[pl.ds(rows_here, W)], v.at[pl.ds(0, W)], halo_send.at[2 * degree], halo_recv.at[2 * degree], row=up)
        )
        halo_down.append(
            remote(
                v.at[pl.ds(W, W)],
                v.at[pl.ds(rows_here + W, W)],
                halo_send.at[2 * degree + 1],
                halo_recv.at[2 * degree + 1],
                row=down,
            )
        )
    halo_up[0].start()
    halo_down[0].start()
    meta_copies = [
        remote(meta_out.at[k, pl.ds(0, 1)], meta_in.at[k, pl.ds(0, 1)], meta_send.at[k], meta_recv.at[k], col=at(*OFF[k]))
        for k in range(1, NB)
    ]
    meta_copies += [
        remote(core_out.at[pl.ds(0, SLOTS)], core_in.at[k, pl.ds(0, SLOTS)], core_send.at[k], core_recv.at[k], col=at(*OFF[k]))
        for k in range(1, NB)
    ]
    for copy in meta_copies:
        copy.start()

    part = 2 * KB // PIECES
    pieces = [(s, half, first) for s in range(CAP) for half in range(2) for first in range(0, KB, part)]

    def send_pieces(s, half, first):
        for k in range(1, NB):
            i = s * NB + k
            remote(
                outgoing.at[i, half, pl.ds(first, part)],
                incoming.at[i, half, pl.ds(first, part)],
                basis_send.at[i],
                basis_recv.at[i],
                col=at(*OFF[k]),
            ).start()

    load_basis.wait()
    for s in range(CAP):
        incoming[s * NB] = basis_vm[owner[s * NB]]

        def pack(k, carry, s=s):
            outgoing[s * NB + k] = basis_vm[owner[s * NB + k]]
            return carry

        lax.fori_loop(1, NB, pack, 0)
        if s == 0:
            for piece in pieces[:EARLY]:
                send_pieces(*piece)

    for side, d in ((0, 1), (1, SIDE - 1)):
        for half, (dy, dz) in enumerate(((0, d), (d, 0))):
            band_wait(half, dy, dz)
            band_part(half, side).start()
    for d in (0, 1, SIDE - 1, 2):
        if d == 2:
            for half in range(2):
                band_part_wait(half, 0)
                band_part_wait(half, 1)
        for other in (1, SIDE - 1):
            band_copy(0, other, d).start()
            band_copy(1, d, other).start()
    for piece in pieces[EARLY : EARLY + 1]:
        send_pieces(*piece)
    for d in range(SIDE):
        near = 1 if d < 2 else SIDE - 1
        band_wait(0, near, d)
        band_copy(0, 2, d).start()
        band_wait(1, d, near)
        band_copy(1, d, 2).start()
    for piece in pieces[EARLY + 1 :]:
        send_pieces(*piece)

    for first in range(SIDE):
        for second in (2, SIDE - 1 if first < 2 else 1):
            band_wait(0, second, first)
            band_wait(1, first, second)

    row_at = lax.broadcasted_iota(jnp.int32, (W, W), 0)
    col_at = lax.broadcasted_iota(jnp.int32, (W, W), 1)

    def build(j, carry):
        coupling = bands[1, j].astype(jnp.float32)
        first = jnp.where((j == 0) & (r == 0), 0.0, 1.0)
        last = jnp.where((j == NB - 1) & (r == rows - 1), 0.0, 1.0)
        band[j, :, 0:W] = (jnp.where(col_at >= row_at, coupling, 0.0) * first).astype(jnp.bfloat16)
        band[j, :, W : 2 * W] = bands[0, j]
        band[j, :, 2 * W : 3 * W] = (jnp.where(col_at < row_at, coupling, 0.0) * last).astype(jnp.bfloat16)
        return carry

    lax.fori_loop(0, NB, build, 0)

    def apply(j, v):
        window = v[pl.ds(pl.multiple_of(j * W, W), 3 * W), :]
        return jnp.dot(band[j], window, preferred_element_type=jnp.float32)

    def inner(j):
        return pl.ds(pl.multiple_of((j + 1) * W, W), W)

    def degree_1(j, carry):
        value = apply(j, v0)
        total[j] = value
        v1[inner(j), :] = value.astype(jnp.bfloat16)
        return carry

    c0, c1, c2, c3 = (coef[i] for i in range(4))

    def degree_2(j, carry):
        start = v0[inner(j), :].astype(jnp.float32)
        value = 2.0 * apply(j, v1) - start
        v2[inner(j), :] = value.astype(jnp.bfloat16)
        total[j] = c0 * start + (c1 - c3) * total[j] + c2 * value
        return carry

    def degree_3(j, carry):
        value = total[j] + (2.0 * c3) * apply(j, v2)
        kern[j // 2, pl.ds(pl.multiple_of(lax.rem(j, 2) * W, W), W), :] = value.astype(jnp.bfloat16)
        return carry

    load_columns.wait()
    halo_up[0].wait()
    halo_down[0].wait()
    for step, degree in ((degree_1, 1), (degree_2, 2)):
        step(0, 0)
        step(NB - 1, 0)
        lax.fori_loop(1, NB // 2, step, 0)
        halo_up[degree].start()
        halo_down[degree].start()
        lax.fori_loop(NB // 2, NB - 1, step, 0)
        halo_up[degree].wait()
        halo_down[degree].wait()
    lax.fori_loop(0, NB, degree_3, 0)

    for half, skip in enumerate(((0, 2), (2, 0))):
        for dy, dz in OFFSETS:
            if (dy, dz) != skip:
                band_copy(half, dy, dz).wait_send()
        for side in range(2):
            band_part(half, side).wait_send()
    for copy in meta_copies:
        copy.wait()
    meta_copy = pltpu.make_async_copy(meta_in.at[:, pl.ds(0, 1)], meta_sm.at[:, pl.ds(0, 1)], local_sem.at[4])
    meta_copy.start()
    meta_copy.wait()
    for s in range(CAP):
        for k in range(NB):
            block_of[s * NB + k] = meta_sm[k, 0, ENTRIES + s]

    def basis_copy(i):
        return remote(outgoing.at[i], incoming.at[i], basis_send.at[i], basis_recv.at[i], col=at(0, 1))

    def project(s, k):
        i = s * NB + k
        keep = pltpu.make_async_copy(incoming.at[i], received.at[i], out_sem.at[i])
        keep.start()
        block = jnp.maximum(meta_sm[k, 0, ENTRIES + s], 0)
        product = jnp.dot(kern[block], incoming[i, 1], preferred_element_type=jnp.float32)
        return jnp.sum(product * incoming[i, 0].astype(jnp.float32), axis=0, keepdims=True) * (1.0 / KB)

    contrib_copies = []
    groups = ((0, 0, NB), (1, 0, NB // 2), (1, NB // 2, NB))
    for g, (s, begin, end) in enumerate(groups):
        if begin == 0:
            contrib[c, s * NB : s * NB + 1, :] = project(s, 0)

        def step(k, carry, s=s):
            basis_copy(s * NB + k).wait_recv()
            contrib[c, pl.ds(s * NB + k, 1), :] = project(s, k)
            return carry

        lax.fori_loop(max(begin, 1), end, step, 0)
        rows_of = pl.ds(s * NB + begin, end - begin)
        lines = contrib.at[c, rows_of]
        for k in range(1, NB):
            i = g * NB + k
            copy = remote(lines, lines, contrib_send.at[i], contrib_recv.at[i], col=at(*OFF[k]))
            copy.start()
            contrib_copies.append(copy)
    def finish(k, carry):
        for s in range(CAP):
            basis_copy(s * NB + k).wait_send()
        return carry

    lax.fori_loop(1, NB, finish, 0)

    def kept(i, carry):
        pltpu.make_async_copy(incoming.at[i], received.at[i], out_sem.at[i]).wait()
        return carry

    lax.fori_loop(0, CAP * NB, kept, 0)

    for g, (s, begin, end) in enumerate(groups):
        for k in range(1, NB):
            i = g * NB + k
            lines = contrib.at[at(-OFF[k][0], -OFF[k][1]), pl.ds(s * NB + begin, end - begin)]
            remote(lines, lines, contrib_send.at[i], contrib_recv.at[i], col=at(0, 1)).wait_recv()

    for copy in contrib_copies:
        copy.wait_send()

    def density_of(k, tile):
        value = core_in[k, pl.ds(tile, 1), :]
        for slot in range(SLOTS):
            place = meta_sm[k, 0, tile * SLOTS + slot]
            there = jnp.maximum(place, 0)
            line = contrib[lax.div(there, CAP * NB), pl.ds(lax.rem(there, CAP * NB), 1), :]
            value = value + jnp.where(place >= 0, line, 0.0)
        return value

    for t in range(ENTRIES // SLOTS):
        dens[t : t + 1, :] = density_of(0, t)

    def slot_density(k, carry):
        for s in range(CAP):
            tile_density[pl.ds(s * NB + k, 1), :] = density_of(k, meta_sm[k, 0, ENTRIES + CAP + s])
        return carry

    lax.fori_loop(0, NB, slot_density, 0, unroll=True)
    x = jnp.maximum(tile_density[...], 0.1)
    root = jnp.exp(jnp.log(x) * (1.0 / 3.0))
    root = root - (root * root * root - x) / (3.0 * root * root)
    pot_in[...] = -exchange_factor * root


def exchange(columns, ham, pattern, coef, peers, tile_block, tile_count, basis, core):
    any_spec = pl.BlockSpec(memory_space=pl.ANY)
    smem = pl.BlockSpec(memory_space=pltpu.SMEM)
    vmem = pl.BlockSpec(memory_space=pltpu.VMEM)
    rows_here = NB * W
    slots = CAP * NB
    bf16, f32, i32 = jnp.bfloat16, jnp.float32, jnp.int32
    dma = pltpu.SemaphoreType.DMA
    return pl.pallas_call(
        exchange_kernel,
        out_shape=(
            jax.ShapeDtypeStruct(core.shape, f32),
            jax.ShapeDtypeStruct((slots, 2, KB, P_SIZE), bf16),
            jax.ShapeDtypeStruct((slots, P_SIZE), f32),
            jax.ShapeDtypeStruct((slots,), i32),
        ),
        in_specs=[any_spec] * 9,
        out_specs=(vmem, any_spec, vmem, smem),
        scratch_shapes=[
            pltpu.SMEM((1,), i32),
            pltpu.SMEM(coef.shape, f32),
            pltpu.SMEM(peers.shape, i32),
            pltpu.SMEM(tile_block.shape, i32),
            pltpu.SMEM(tile_count.shape, i32),
            pltpu.VMEM(core.shape, f32),
            pltpu.VMEM((W, W), bf16),
            pltpu.VMEM((2, NB, W, W), bf16),
            pltpu.VMEM((NB, W, 3 * W), bf16),
            pltpu.VMEM((rows_here + 2 * W, KB), bf16),
            pltpu.VMEM((rows_here + 2 * W, KB), bf16),
            pltpu.VMEM((rows_here + 2 * W, KB), bf16),
            pltpu.VMEM((NB, W, KB), f32),
            pltpu.VMEM((rows_here // KB, KB, KB), bf16),
            pltpu.VMEM(basis.shape, bf16),
            pltpu.VMEM((slots, 2, KB, P_SIZE), bf16),
            pltpu.VMEM((slots, 2, KB, P_SIZE), bf16),
            pltpu.VMEM((NB, 8, P_SIZE), i32),
            pltpu.VMEM((NB, 8, P_SIZE), i32),
            pltpu.SMEM((NB, 8, P_SIZE), i32),
            pltpu.VMEM((8, P_SIZE), f32),
            pltpu.VMEM((NB, 8, P_SIZE), f32),
            pltpu.VMEM((NB, slots, P_SIZE), f32),
            pltpu.VMEM((slots, P_SIZE), f32),
            pltpu.SMEM((slots,), i32),
            dma((11,)),
            dma((slots,)),
            dma((2 * (NB - 1) + 4,)),
            dma((2 * (NB - 1) + 4,)),
            dma((NB,)),
            dma((NB,)),
            dma((6,)),
            dma((6,)),
            dma((slots,)),
            dma((slots,)),
            dma((3 * NB,)),
            dma((3 * NB,)),
            dma((NB,)),
            dma((NB,)),
        ],
        compiler_params=pltpu.CompilerParams(
            collective_id=0, has_side_effects=True, vmem_limit_bytes=66_000_000
        ),
        name="exchange",
    )(columns, ham, pattern, coef, peers, tile_block, tile_count, basis, core)


def update_kernel(
    received, pot, block_of, density, out, dens, pairs, lines, blocks, named, count, total, rounded, points, pair_sem, sem
):
    slots = CAP * NB
    row_blocks = NB * W // KB
    load_blocks = pltpu.make_async_copy(block_of, blocks, sem.at[0])
    load_lines = pltpu.make_async_copy(pot, lines, sem.at[1])
    load_blocks.start()
    load_lines.start()
    load_points = pltpu.make_async_copy(density, points, sem.at[2 + row_blocks])
    store_points = pltpu.make_async_copy(points, dens, sem.at[3 + row_blocks])
    load_points.start()
    for b in range(row_blocks):
        count[b] = 0
    load_blocks.wait()

    def load(i):
        return pltpu.make_async_copy(received.at[i], pairs.at[i], pair_sem.at[i])

    def sort(i, carry):
        block = blocks[i]

        @pl.when(block >= 0)
        def _():
            named[block * slots + count[block]] = i
            count[block] = count[block] + 1

        return carry

    lax.fori_loop(0, slots, sort, 0)

    def fetch(b, carry):
        def one(j, carry):
            load(named[b * slots + j]).start()
            return carry

        return lax.fori_loop(0, count[b], one, carry)

    lax.fori_loop(0, row_blocks, fetch, 0)
    load_lines.wait()
    load_points.wait()
    store_points.start()

    def store(b):
        return pltpu.make_async_copy(rounded.at[b], out.at[b], sem.at[2 + b])

    def weighted(i, present):
        line = jnp.where(present, lines[pl.ds(i, 1), :], 0.0)
        return (pairs[i, 1].astype(jnp.float32) * line).astype(jnp.bfloat16)

    def product(b, j, n, group):
        first = named[b * slots + group * j]
        left, right = [], []
        for q in range(group):
            here = group * j + q < n
            i = jnp.where(here, named[b * slots + group * j + q], first)

            @pl.when(here)
            def _(i=i):
                load(i).wait()

            left.append(i)
            right.append(here)
        return lax.dot_general(
            jnp.concatenate([pairs[i, 0] for i in left], axis=1),
            jnp.concatenate([weighted(i, here) for i, here in zip(left, right)], axis=1),
            (((1,), (1,)), ((), ())),
            preferred_element_type=jnp.float32,
        )

    scale = 1.0 / math.sqrt(P_SIZE)

    def block_sum(b, carry):
        n = count[b]

        for fewer, group in ((0, 2), (2, GROUP)):

            @pl.when((n > fewer) & (n <= group))
            def _(group=group):
                rounded[b] = (product(b, 0, n, group) * scale).astype(jnp.bfloat16)

        @pl.when(n > GROUP)
        def _():
            total[...] = jnp.zeros_like(total)

            def add(j, carry):
                total[...] = total[...] + product(b, j, n, GROUP)
                return carry

            lax.fori_loop(0, lax.div(n + GROUP - 1, GROUP), add, 0)
            rounded[b] = (total[...] * scale).astype(jnp.bfloat16)

        @pl.when(n > 0)
        def _():
            store(b).start()

        return carry

    def clear(b, carry):
        @pl.when(count[b] == 0)
        def _():
            rounded[b] = jnp.zeros((KB, KB), jnp.bfloat16)
            store(b).start()

        return carry

    lax.fori_loop(0, row_blocks, clear, 0)
    lax.fori_loop(0, row_blocks, block_sum, 0)
    for b in range(row_blocks):
        store(b).wait()
    store_points.wait()


def update(block_of, received, pot_in, density):
    blocks = NB * W // KB
    any_spec = pl.BlockSpec(memory_space=pl.ANY)
    return pl.pallas_call(
        update_kernel,
        out_shape=(
            jax.ShapeDtypeStruct((blocks, KB, KB), jnp.bfloat16),
            jax.ShapeDtypeStruct(density.shape, density.dtype),
        ),
        in_specs=[any_spec] * 4,
        out_specs=(any_spec, any_spec),
        scratch_shapes=[
            pltpu.VMEM(received.shape, received.dtype),
            pltpu.VMEM(pot_in.shape, pot_in.dtype),
            pltpu.SMEM(block_of.shape, block_of.dtype),
            pltpu.SMEM((blocks * CAP * NB,), jnp.int32),
            pltpu.SMEM((blocks,), jnp.int32),
            pltpu.VMEM((KB, KB), jnp.float32),
            pltpu.VMEM((blocks, KB, KB), jnp.bfloat16),
            pltpu.VMEM(density.shape, density.dtype),
            pltpu.SemaphoreType.DMA((CAP * NB,)),
            pltpu.SemaphoreType.DMA((4 + blocks,)),
        ],
        compiler_params=pltpu.CompilerParams(vmem_limit_bytes=67_000_000),
        name="update",
    )(received, pot_in, block_of, density)


def shards(columns, ham, pattern, coef, peers, tile_block, tile_count, basis, core):
    dens, received, pot_in, block_of = exchange(
        columns, ham, pattern, coef, peers.reshape(-1), tile_block, tile_count, basis, core
    )
    blocks, dens = update(block_of, received, pot_in, dens)
    return dens, blocks.reshape(columns.shape)


def solution(mesh):
    return jax.shard_map(
        shards,
        mesh=mesh,
        in_specs=(
            P("row", "col"),
            P(("row", "col"), None, None, None),
            P(("row", "col")),
            P(),
            P(("row", "col"), None),
            P(("row", "col")),
            P(("row", "col")),
            P(("row", "col"), None, None, None),
            P(("row", "col"), None),
        ),
        out_specs=(P(("row", "col"), None), P("row", "col")),
        check_vma=False,
    )
```

```python
import functools
import math

import jax
import jax.numpy as jnp
from jax import lax
from jax.experimental import pallas as pl
from jax.experimental.pallas import tpu as pltpu
from jax.sharding import PartitionSpec as P

MESH = pl.DeviceIdType.MESH
W = 256
KB = 512
SLOTS = 4
CAP = 2
P_SIZE = 128
GROUP = 4
NB = 16
ENTRIES = 16
PIECES = 8
EARLY = 1
SIDE = 4
OFFSETS = tuple((k // SIDE, k % SIDE) for k in range(1, NB))


def hops(offset):
    return sum(min(d, SIDE - d) for d in offset)


FAR = sorted(OFFSETS, key=hops, reverse=True)
OFF = ((0, 0),) + tuple(FAR[i // 2] if i % 2 == 0 else FAR[-1 - i // 2] for i in range(NB - 1))

exchange_factor = (3.0 / math.pi) ** (1.0 / 3.0)


def exchange_kernel(
    columns,
    ham,
    pattern,
    coef_at,
    peers_at,
    block_at,
    count_at,
    basis,
    core_at,
    dens,
    received,
    pot_in,
    block_of,
    present,
    coef,
    peers,
    tile_block,
    tile_count,
    core,
    own_ham,
    bands,
    band,
    v0,
    v1,
    v2,
    total,
    kern,
    basis_vm,
    outgoing,
    incoming,
    meta_out,
    meta_in,
    meta_sm,
    core_out,
    core_in,
    contrib,
    tile_density,
    owner,
    local_sem,
    out_sem,
    band_send,
    band_recv,
    meta_send,
    meta_recv,
    halo_send,
    halo_recv,
    basis_send,
    basis_recv,
    contrib_send,
    contrib_recv,
    core_send,
    core_recv,
):
    r = lax.axis_index("row")
    c = lax.axis_index("col")
    rows = lax.axis_size("row")
    y, z = c // SIDE, c % SIDE
    rows_here = NB * W

    def at(dy, dz):
        return lax.rem(y + dy + SIDE, SIDE) * SIDE + lax.rem(z + dz + SIDE, SIDE)

    def remote(src, dst, send, recv, **where):
        return pltpu.make_async_remote_copy(
            src_ref=src, dst_ref=dst, send_sem=send, recv_sem=recv, device_id=where, device_id_type=MESH
        )

    up, down = lax.rem(r + 1, rows), lax.rem(r + rows - 1, rows)

    barrier = pltpu.get_barrier_semaphore()
    for dy, dz in OFFSETS:
        pl.semaphore_signal(barrier, inc=1, device_id={"col": at(dy, dz)}, device_id_type=MESH)
    for row in (up, down):
        pl.semaphore_signal(barrier, inc=1, device_id={"row": row}, device_id_type=MESH)

    load_diag = pltpu.make_async_copy(ham.at[0, 0], bands.at[0, c], local_sem.at[0])
    load_coupling = pltpu.make_async_copy(ham.at[0, 1], own_ham, local_sem.at[1])
    load_basis = pltpu.make_async_copy(basis, basis_vm, local_sem.at[2])
    load_columns = pltpu.make_async_copy(columns, v0.at[pl.ds(W, rows_here)], local_sem.at[3])
    small = [
        pltpu.make_async_copy(source, target, local_sem.at[5 + i])
        for i, (source, target) in enumerate(
            (
                (peers_at, peers),
                (count_at, tile_count),
                (block_at, tile_block),
                (core_at, core),
                (coef_at, coef),
                (pattern, present),
            )
        )
    ]
    for copy in small:
        copy.start()
    load_diag.start()
    load_coupling.start()
    load_basis.start()
    load_columns.start()

    for copy in small:
        copy.wait()
    core_out[...] = jnp.concatenate([core[...], jnp.zeros_like(core[...])], axis=0)
    core_in[0] = core_out[...]
    lane = lax.broadcasted_iota(jnp.int32, (8, P_SIZE), 1)
    codes = jnp.full((8, P_SIZE), -1, jnp.int32)
    slots_of = []
    for k in range(NB):
        peer = at(*OFF[k])
        first, second = jnp.int32(ENTRIES), jnp.int32(ENTRIES)
        for e in reversed(range(ENTRIES)):
            named = peers[e] == peer
            second = jnp.where(named, first, second)
            first = jnp.where(named, jnp.int32(e), first)
        fields = []
        for s, found in enumerate((first, second)):
            entry = jnp.minimum(found, ENTRIES - 1)
            live = (found < ENTRIES) & (lax.rem(entry, SLOTS) < tile_count[lax.div(entry, SLOTS)])
            owner[s * NB + k] = entry
            fields.append((jnp.where(live, tile_block[entry], -1), lax.div(entry, SLOTS)))
            codes = jnp.where((lane == entry) & live, peer * (CAP * NB) + s * NB + k, codes)
        slots_of.append(fields)
    for k in range(NB):
        words = codes
        for s in range(CAP):
            words = jnp.where(lane == ENTRIES + s, slots_of[k][s][0], words)
            words = jnp.where(lane == ENTRIES + CAP + s, slots_of[k][s][1], words)
        if k == 0:
            meta_in[0] = words
        else:
            meta_out[k] = words

    load_coupling.wait()
    bands[1, c] = (own_ham[...].astype(jnp.float32) * present[0].astype(jnp.float32)).astype(jnp.bfloat16)
    load_diag.wait()
    pl.semaphore_wait(barrier, NB - 1 + 2)

    def band_copy(half, dy, dz):
        first, second = (dz, dy) if half == 0 else (dy, dz)
        done, hop = (first, second) if second else (0, first)
        before = 0
        if second == 2:
            hop, before = (1, 1) if first < 2 else (-1, -1)
        if half == 0:
            source, there = at(-before, -done), (at(hop, 0) if second else at(0, hop))
        else:
            source, there = at(-done, -before), (at(0, hop) if second else at(hop, 0))
        i = half * (NB - 1) + dy * SIDE + dz - 1
        return remote(bands.at[half, source], bands.at[half, source], band_send.at[i], band_recv.at[i], col=there)

    def band_wait(half, dy, dz):
        i = half * (NB - 1) + dy * SIDE + dz - 1
        block = bands.at[half, at(-dy, -dz)]
        remote(block, block, band_send.at[i], band_recv.at[i], col=at(dy, dz)).wait_recv()

    def band_part(half, side):
        hop = 1 - 2 * side
        along = (lambda step: at(0, step)) if half == 0 else (lambda step: at(step, 0))
        part = bands.at[half, along(-hop), pl.ds(side * (W // 2), W // 2)]
        i = 2 * (NB - 1) + 2 * half + side
        return remote(part, part, band_send.at[i], band_recv.at[i], col=along(hop))

    def band_part_wait(half, side):
        along = (lambda step: at(0, step)) if half == 0 else (lambda step: at(step, 0))
        part = bands.at[half, along(2), pl.ds(side * (W // 2), W // 2)]
        i = 2 * (NB - 1) + 2 * half + side
        remote(part, part, band_send.at[i], band_recv.at[i], col=along(1)).wait_recv()

    for d in (1, SIDE - 1):
        band_copy(0, 0, d).start()
        band_copy(1, d, 0).start()
    halo_up = [remote(columns.at[pl.ds(rows_here - W, W)], v0.at[pl.ds(0, W)], halo_send.at[0], halo_recv.at[0], row=up)]
    halo_down = [remote(columns.at[pl.ds(0, W)], v0.at[pl.ds(rows_here + W, W)], halo_send.at[1], halo_recv.at[1], row=down)]
    for degree, v in ((1, v1), (2, v2)):
        halo_up.append(
            remote(v.at[pl.ds(rows_here, W)], v.at[pl.ds(0, W)], halo_send.at[2 * degree], halo_recv.at[2 * degree], row=up)
        )
        halo_down.append(
            remote(
                v.at[pl.ds(W, W)],
                v.at[pl.ds(rows_here + W, W)],
                halo_send.at[2 * degree + 1],
                halo_recv.at[2 * degree + 1],
                row=down,
            )
        )
    halo_up[0].start()
    halo_down[0].start()
    meta_copies = [
        remote(meta_out.at[k, pl.ds(0, 1)], meta_in.at[k, pl.ds(0, 1)], meta_send.at[k], meta_recv.at[k], col=at(*OFF[k]))
        for k in range(1, NB)
    ]
    meta_copies += [
        remote(core_out.at[pl.ds(0, SLOTS)], core_in.at[k, pl.ds(0, SLOTS)], core_send.at[k], core_recv.at[k], col=at(*OFF[k]))
        for k in range(1, NB)
    ]
    for copy in meta_copies:
        copy.start()

    part = 2 * KB // PIECES
    pieces = [(s, half, first) for s in range(CAP) for half in range(2) for first in range(0, KB, part)]

    def send_pieces(s, half, first):
        for k in range(1, NB):
            i = s * NB + k
            remote(
                outgoing.at[i, half, pl.ds(first, part)],
                incoming.at[i, half, pl.ds(first, part)],
                basis_send.at[i],
                basis_recv.at[i],
                col=at(*OFF[k]),
            ).start()

    load_basis.wait()
    for s in range(CAP):
        incoming[s * NB] = basis_vm[owner[s * NB]]

        def pack(k, carry, s=s):
            outgoing[s * NB + k] = basis_vm[owner[s * NB + k]]
            return carry

        lax.fori_loop(1, NB, pack, 0)
        if s == 0:
            for piece in pieces[:EARLY]:
                send_pieces(*piece)

    for side, d in ((0, 1), (1, SIDE - 1)):
        for half, (dy, dz) in enumerate(((0, d), (d, 0))):
            band_wait(half, dy, dz)
            band_part(half, side).start()
    for d in (0, 1, SIDE - 1, 2):
        if d == 2:
            for half in range(2):
                band_part_wait(half, 0)
                band_part_wait(half, 1)
        for other in (1, SIDE - 1):
            band_copy(0, other, d).start()
            band_copy(1, d, other).start()
    for piece in pieces[EARLY : EARLY + 1]:
        send_pieces(*piece)
    for d in range(SIDE):
        near = 1 if d < 2 else SIDE - 1
        band_wait(0, near, d)
        band_copy(0, 2, d).start()
        band_wait(1, d, near)
        band_copy(1, d, 2).start()
    for piece in pieces[EARLY + 1 :]:
        send_pieces(*piece)

    for first in range(SIDE):
        for second in (2, SIDE - 1 if first < 2 else 1):
            band_wait(0, second, first)
            band_wait(1, first, second)

    row_at = lax.broadcasted_iota(jnp.int32, (W, W), 0)
    col_at = lax.broadcasted_iota(jnp.int32, (W, W), 1)

    def build(j, carry):
        coupling = bands[1, j].astype(jnp.float32)
        first = jnp.where((j == 0) & (r == 0), 0.0, 1.0)
        last = jnp.where((j == NB - 1) & (r == rows - 1), 0.0, 1.0)
        band[j, :, 0:W] = (jnp.where(col_at >= row_at, coupling, 0.0) * first).astype(jnp.bfloat16)
        band[j, :, W : 2 * W] = bands[0, j]
        band[j, :, 2 * W : 3 * W] = (jnp.where(col_at < row_at, coupling, 0.0) * last).astype(jnp.bfloat16)
        return carry

    lax.fori_loop(0, NB, build, 0)

    def apply(j, v):
        window = v[pl.ds(pl.multiple_of(j * W, W), 3 * W), :]
        return jnp.dot(band[j], window, preferred_element_type=jnp.float32)

    def inner(j):
        return pl.ds(pl.multiple_of((j + 1) * W, W), W)

    def degree_1(j, carry):
        value = apply(j, v0)
        total[j] = value
        v1[inner(j), :] = value.astype(jnp.bfloat16)
        return carry

    c0, c1, c2, c3 = (coef[i] for i in range(4))

    def degree_2(j, carry):
        start = v0[inner(j), :].astype(jnp.float32)
        value = 2.0 * apply(j, v1) - start
        v2[inner(j), :] = value.astype(jnp.bfloat16)
        total[j] = c0 * start + (c1 - c3) * total[j] + c2 * value
        return carry

    def degree_3(j, carry):
        value = total[j] + (2.0 * c3) * apply(j, v2)
        kern[j // 2, pl.ds(pl.multiple_of(lax.rem(j, 2) * W, W), W), :] = value.astype(jnp.bfloat16)
        return carry

    load_columns.wait()
    halo_up[0].wait()
    halo_down[0].wait()
    for step, degree in ((degree_1, 1), (degree_2, 2)):
        step(0, 0)
        step(NB - 1, 0)
        lax.fori_loop(1, NB // 2, step, 0)
        halo_up[degree].start()
        halo_down[degree].start()
        lax.fori_loop(NB // 2, NB - 1, step, 0)
        halo_up[degree].wait()
        halo_down[degree].wait()
    lax.fori_loop(0, NB, degree_3, 0)

    for half, skip in enumerate(((0, 2), (2, 0))):
        for dy, dz in OFFSETS:
            if (dy, dz) != skip:
                band_copy(half, dy, dz).wait_send()
        for side in range(2):
            band_part(half, side).wait_send()
    for copy in meta_copies:
        copy.wait()
    meta_copy = pltpu.make_async_copy(meta_in.at[:, pl.ds(0, 1)], meta_sm.at[:, pl.ds(0, 1)], local_sem.at[4])
    meta_copy.start()
    meta_copy.wait()
    for s in range(CAP):
        for k in range(NB):
            block_of[s * NB + k] = meta_sm[k, 0, ENTRIES + s]

    def basis_copy(i):
        return remote(outgoing.at[i], incoming.at[i], basis_send.at[i], basis_recv.at[i], col=at(0, 1))

    def project(s, k):
        i = s * NB + k
        keep = pltpu.make_async_copy(incoming.at[i], received.at[i], out_sem.at[i])
        keep.start()
        block = jnp.maximum(meta_sm[k, 0, ENTRIES + s], 0)
        product = jnp.dot(kern[block], incoming[i, 1], preferred_element_type=jnp.float32)
        return jnp.sum(product * incoming[i, 0].astype(jnp.float32), axis=0, keepdims=True) * (1.0 / KB)

    contrib_copies = []
    groups = ((0, 0, NB), (1, 0, NB // 2), (1, NB // 2, NB))
    for g, (s, begin, end) in enumerate(groups):
        if begin == 0:
            contrib[c, s * NB : s * NB + 1, :] = project(s, 0)

        def step(k, carry, s=s):
            basis_copy(s * NB + k).wait_recv()
            contrib[c, pl.ds(s * NB + k, 1), :] = project(s, k)
            return carry

        lax.fori_loop(max(begin, 1), end, step, 0)
        rows_of = pl.ds(s * NB + begin, end - begin)
        lines = contrib.at[c, rows_of]
        for k in range(1, NB):
            i = g * NB + k
            copy = remote(lines, lines, contrib_send.at[i], contrib_recv.at[i], col=at(*OFF[k]))
            copy.start()
            contrib_copies.append(copy)
    def finish(k, carry):
        for s in range(CAP):
            basis_copy(s * NB + k).wait_send()
        return carry

    lax.fori_loop(1, NB, finish, 0)

    def kept(i, carry):
        pltpu.make_async_copy(incoming.at[i], received.at[i], out_sem.at[i]).wait()
        return carry

    lax.fori_loop(0, CAP * NB, kept, 0)

    for g, (s, begin, end) in enumerate(groups):
        for k in range(1, NB):
            i = g * NB + k
            lines = contrib.at[at(-OFF[k][0], -OFF[k][1]), pl.ds(s * NB + begin, end - begin)]
            remote(lines, lines, contrib_send.at[i], contrib_recv.at[i], col=at(0, 1)).wait_recv()

    for copy in contrib_copies:
        copy.wait_send()

    def density_of(k, tile):
        value = core_in[k, pl.ds(tile, 1), :]
        for slot in range(SLOTS):
            place = meta_sm[k, 0, tile * SLOTS + slot]
            there = jnp.maximum(place, 0)
            line = contrib[lax.div(there, CAP * NB), pl.ds(lax.rem(there, CAP * NB), 1), :]
            value = value + jnp.where(place >= 0, line, 0.0)
        return value

    for t in range(ENTRIES // SLOTS):
        dens[t : t + 1, :] = density_of(0, t)

    def slot_density(k, carry):
        for s in range(CAP):
            tile_density[pl.ds(s * NB + k, 1), :] = density_of(k, meta_sm[k, 0, ENTRIES + CAP + s])
        return carry

    lax.fori_loop(0, NB, slot_density, 0, unroll=True)
    x = jnp.maximum(tile_density[...], 0.1)
    root = jnp.exp(jnp.log(x) * (1.0 / 3.0))
    root = root - (root * root * root - x) / (3.0 * root * root)
    pot_in[...] = -exchange_factor * root


def exchange(columns, ham, pattern, coef, peers, tile_block, tile_count, basis, core):
    any_spec = pl.BlockSpec(memory_space=pl.ANY)
    smem = pl.BlockSpec(memory_space=pltpu.SMEM)
    vmem = pl.BlockSpec(memory_space=pltpu.VMEM)
    rows_here = NB * W
    slots = CAP * NB
    bf16, f32, i32 = jnp.bfloat16, jnp.float32, jnp.int32
    dma = pltpu.SemaphoreType.DMA
    return pl.pallas_call(
        exchange_kernel,
        out_shape=(
            jax.ShapeDtypeStruct(core.shape, f32),
            jax.ShapeDtypeStruct((slots, 2, KB, P_SIZE), bf16),
            jax.ShapeDtypeStruct((slots, P_SIZE), f32),
            jax.ShapeDtypeStruct((slots,), i32),
        ),
        in_specs=[any_spec] * 9,
        out_specs=(vmem, any_spec, vmem, smem),
        scratch_shapes=[
            pltpu.SMEM((1,), i32),
            pltpu.SMEM(coef.shape, f32),
            pltpu.SMEM(peers.shape, i32),
            pltpu.SMEM(tile_block.shape, i32),
            pltpu.SMEM(tile_count.shape, i32),
            pltpu.VMEM(core.shape, f32),
            pltpu.VMEM((W, W), bf16),
            pltpu.VMEM((2, NB, W, W), bf16),
            pltpu.VMEM((NB, W, 3 * W), bf16),
            pltpu.VMEM((rows_here + 2 * W, KB), bf16),
            pltpu.VMEM((rows_here + 2 * W, KB), bf16),
            pltpu.VMEM((rows_here + 2 * W, KB), bf16),
            pltpu.VMEM((NB, W, KB), f32),
            pltpu.VMEM((rows_here // KB, KB, KB), bf16),
            pltpu.VMEM(basis.shape, bf16),
            pltpu.VMEM((slots, 2, KB, P_SIZE), bf16),
            pltpu.VMEM((slots, 2, KB, P_SIZE), bf16),
            pltpu.VMEM((NB, 8, P_SIZE), i32),
            pltpu.VMEM((NB, 8, P_SIZE), i32),
            pltpu.SMEM((NB, 8, P_SIZE), i32),
            pltpu.VMEM((8, P_SIZE), f32),
            pltpu.VMEM((NB, 8, P_SIZE), f32),
            pltpu.VMEM((NB, slots, P_SIZE), f32),
            pltpu.VMEM((slots, P_SIZE), f32),
            pltpu.SMEM((slots,), i32),
            dma((11,)),
            dma((slots,)),
            dma((2 * (NB - 1) + 4,)),
            dma((2 * (NB - 1) + 4,)),
            dma((NB,)),
            dma((NB,)),
            dma((6,)),
            dma((6,)),
            dma((slots,)),
            dma((slots,)),
            dma((3 * NB,)),
            dma((3 * NB,)),
            dma((NB,)),
            dma((NB,)),
        ],
        compiler_params=pltpu.CompilerParams(
            collective_id=0, has_side_effects=True, vmem_limit_bytes=66_000_000
        ),
        name="exchange",
    )(columns, ham, pattern, coef, peers, tile_block, tile_count, basis, core)


def update_kernel(
    received, pot, block_of, density, out, dens, pairs, lines, blocks, named, count, total, rounded, points, pair_sem, sem
):
    slots = CAP * NB
    row_blocks = NB * W // KB
    load_blocks = pltpu.make_async_copy(block_of, blocks, sem.at[0])
    load_lines = pltpu.make_async_copy(pot, lines, sem.at[1])
    load_blocks.start()
    load_lines.start()
    load_points = pltpu.make_async_copy(density, points, sem.at[2 + row_blocks])
    store_points = pltpu.make_async_copy(points, dens, sem.at[3 + row_blocks])
    load_points.start()
    for b in range(row_blocks):
        count[b] = 0
    load_blocks.wait()

    def load(i):
        return pltpu.make_async_copy(received.at[i], pairs.at[i], pair_sem.at[i])

    def sort(i, carry):
        block = blocks[i]

        @pl.when(block >= 0)
        def _():
            named[block * slots + count[block]] = i
            count[block] = count[block] + 1

        return carry

    lax.fori_loop(0, slots, sort, 0)

    def fetch(b, carry):
        def one(j, carry):
            load(named[b * slots + j]).start()
            return carry

        return lax.fori_loop(0, count[b], one, carry)

    lax.fori_loop(0, row_blocks, fetch, 0)
    load_lines.wait()
    load_points.wait()
    store_points.start()

    def store(b):
        return pltpu.make_async_copy(rounded.at[b], out.at[b], sem.at[2 + b])

    def weighted(i, present):
        line = jnp.where(present, lines[pl.ds(i, 1), :], 0.0)
        return (pairs[i, 1].astype(jnp.float32) * line).astype(jnp.bfloat16)

    def product(b, j, n, group):
        first = named[b * slots + group * j]
        left, right = [], []
        for q in range(group):
            here = group * j + q < n
            i = jnp.where(here, named[b * slots + group * j + q], first)

            @pl.when(here)
            def _(i=i):
                load(i).wait()

            left.append(i)
            right.append(here)
        return lax.dot_general(
            jnp.concatenate([pairs[i, 0] for i in left], axis=1),
            jnp.concatenate([weighted(i, here) for i, here in zip(left, right)], axis=1),
            (((1,), (1,)), ((), ())),
            preferred_element_type=jnp.float32,
        )

    scale = 1.0 / math.sqrt(P_SIZE)

    def block_sum(b, carry):
        n = count[b]

        for fewer, group in ((0, 2), (2, GROUP)):

            @pl.when((n > fewer) & (n <= group))
            def _(group=group):
                rounded[b] = (product(b, 0, n, group) * scale).astype(jnp.bfloat16)

        @pl.when(n > GROUP)
        def _():
            total[...] = jnp.zeros_like(total)

            def add(j, carry):
                total[...] = total[...] + product(b, j, n, GROUP)
                return carry

            lax.fori_loop(0, lax.div(n + GROUP - 1, GROUP), add, 0)
            rounded[b] = (total[...] * scale).astype(jnp.bfloat16)

        @pl.when(n > 0)
        def _():
            store(b).start()

        return carry

    def clear(b, carry):
        @pl.when(count[b] == 0)
        def _():
            rounded[b] = jnp.zeros((KB, KB), jnp.bfloat16)
            store(b).start()

        return carry

    lax.fori_loop(0, row_blocks, clear, 0)
    lax.fori_loop(0, row_blocks, block_sum, 0)
    for b in range(row_blocks):
        store(b).wait()
    store_points.wait()


def update(block_of, received, pot_in, density):
    blocks = NB * W // KB
    any_spec = pl.BlockSpec(memory_space=pl.ANY)
    return pl.pallas_call(
        update_kernel,
        out_shape=(
            jax.ShapeDtypeStruct((blocks, KB, KB), jnp.bfloat16),
            jax.ShapeDtypeStruct(density.shape, density.dtype),
        ),
        in_specs=[any_spec] * 4,
        out_specs=(any_spec, any_spec),
        scratch_shapes=[
            pltpu.VMEM(received.shape, received.dtype),
            pltpu.VMEM(pot_in.shape, pot_in.dtype),
            pltpu.SMEM(block_of.shape, block_of.dtype),
            pltpu.SMEM((blocks * CAP * NB,), jnp.int32),
            pltpu.SMEM((blocks,), jnp.int32),
            pltpu.VMEM((KB, KB), jnp.float32),
            pltpu.VMEM((blocks, KB, KB), jnp.bfloat16),
            pltpu.VMEM(density.shape, density.dtype),
            pltpu.SemaphoreType.DMA((CAP * NB,)),
            pltpu.SemaphoreType.DMA((4 + blocks,)),
        ],
        compiler_params=pltpu.CompilerParams(vmem_limit_bytes=67_000_000),
        name="update",
    )(received, pot_in, block_of, density)


def shards(columns, ham, pattern, coef, peers, tile_block, tile_count, basis, core):
    dens, received, pot_in, block_of = exchange(
        columns, ham, pattern, coef, peers.reshape(-1), tile_block, tile_count, basis, core
    )
    blocks, dens = update(block_of, received, pot_in, dens)
    return dens, blocks.reshape(columns.shape)


def solution(mesh):
    return jax.shard_map(
        shards,
        mesh=mesh,
        in_specs=(
            P("row", "col"),
            P(("row", "col"), None, None, None),
            P(("row", "col")),
            P(),
            P(("row", "col"), None),
            P(("row", "col")),
            P(("row", "col")),
            P(("row", "col"), None, None, None),
            P(("row", "col"), None),
        ),
        out_specs=(P(("row", "col"), None), P("row", "col")),
        check_vma=False,
    )
```

```python
import functools
import math

import jax
import jax.numpy as jnp
from jax import lax
from jax.experimental import pallas as pl
from jax.experimental.pallas import tpu as pltpu
from jax.sharding import PartitionSpec as P

MESH = pl.DeviceIdType.MESH
W = 256
KB = 512
SLOTS = 4
CAP = 2
P_SIZE = 128
GROUP = 4
NB = 16
ENTRIES = 16
PIECES = 8
EARLY = 0
SIDE = 4
OFFSETS = tuple((k // SIDE, k % SIDE) for k in range(1, NB))


def hops(offset):
    return sum(min(d, SIDE - d) for d in offset)


FAR = sorted(OFFSETS, key=hops, reverse=True)
OFF = ((0, 0),) + tuple(FAR[i // 2] if i % 2 == 0 else FAR[-1 - i // 2] for i in range(NB - 1))

exchange_factor = (3.0 / math.pi) ** (1.0 / 3.0)


def exchange_kernel(
    columns,
    ham,
    pattern,
    coef_at,
    peers_at,
    block_at,
    count_at,
    basis,
    core_at,
    dens,
    received,
    pot_in,
    block_of,
    present,
    coef,
    peers,
    tile_block,
    tile_count,
    core,
    own_ham,
    bands,
    band,
    v0,
    v1,
    v2,
    total,
    kern,
    basis_vm,
    outgoing,
    incoming,
    meta_out,
    meta_in,
    meta_sm,
    core_out,
    core_in,
    contrib,
    tile_density,
    owner,
    local_sem,
    out_sem,
    band_send,
    band_recv,
    meta_send,
    meta_recv,
    halo_send,
    halo_recv,
    basis_send,
    basis_recv,
    contrib_send,
    contrib_recv,
    core_send,
    core_recv,
):
    r = lax.axis_index("row")
    c = lax.axis_index("col")
    rows = lax.axis_size("row")
    y, z = c // SIDE, c % SIDE
    rows_here = NB * W

    def at(dy, dz):
        return lax.rem(y + dy + SIDE, SIDE) * SIDE + lax.rem(z + dz + SIDE, SIDE)

    def remote(src, dst, send, recv, **where):
        return pltpu.make_async_remote_copy(
            src_ref=src, dst_ref=dst, send_sem=send, recv_sem=recv, device_id=where, device_id_type=MESH
        )

    up, down = lax.rem(r + 1, rows), lax.rem(r + rows - 1, rows)

    barrier = pltpu.get_barrier_semaphore()
    for dy, dz in OFFSETS:
        pl.semaphore_signal(barrier, inc=1, device_id={"col": at(dy, dz)}, device_id_type=MESH)
    for row in (up, down):
        pl.semaphore_signal(barrier, inc=1, device_id={"row": row}, device_id_type=MESH)

    load_diag = pltpu.make_async_copy(ham.at[0, 0], bands.at[0, c], local_sem.at[0])
    load_coupling = pltpu.make_async_copy(ham.at[0, 1], own_ham, local_sem.at[1])
    load_basis = pltpu.make_async_copy(basis, basis_vm, local_sem.at[2])
    load_columns = pltpu.make_async_copy(columns, v0.at[pl.ds(W, rows_here)], local_sem.at[3])
    small = [
        pltpu.make_async_copy(source, target, local_sem.at[5 + i])
        for i, (source, target) in enumerate(
            (
                (peers_at, peers),
                (count_at, tile_count),
                (block_at, tile_block),
                (core_at, core),
                (coef_at, coef),
                (pattern, present),
            )
        )
    ]
    for copy in small:
        copy.start()
    load_diag.start()
    load_coupling.start()
    load_basis.start()
    load_columns.start()

    for copy in small:
        copy.wait()
    core_out[...] = jnp.concatenate([core[...], jnp.zeros_like(core[...])], axis=0)
    core_in[0] = core_out[...]
    lane = lax.broadcasted_iota(jnp.int32, (8, P_SIZE), 1)
    codes = jnp.full((8, P_SIZE), -1, jnp.int32)
    slots_of = []
    for k in range(NB):
        peer = at(*OFF[k])
        first, second = jnp.int32(ENTRIES), jnp.int32(ENTRIES)
        for e in reversed(range(ENTRIES)):
            named = peers[e] == peer
            second = jnp.where(named, first, second)
            first = jnp.where(named, jnp.int32(e), first)
        fields = []
        for s, found in enumerate((first, second)):
            entry = jnp.minimum(found, ENTRIES - 1)
            live = (found < ENTRIES) & (lax.rem(entry, SLOTS) < tile_count[lax.div(entry, SLOTS)])
            owner[s * NB + k] = entry
            fields.append((jnp.where(live, tile_block[entry], -1), lax.div(entry, SLOTS)))
            codes = jnp.where((lane == entry) & live, peer * (CAP * NB) + s * NB + k, codes)
        slots_of.append(fields)
    for k in range(NB):
        words = codes
        for s in range(CAP):
            words = jnp.where(lane == ENTRIES + s, slots_of[k][s][0], words)
            words = jnp.where(lane == ENTRIES + CAP + s, slots_of[k][s][1], words)
        if k == 0:
            meta_in[0] = words
        else:
            meta_out[k] = words

    load_coupling.wait()
    bands[1, c] = (own_ham[...].astype(jnp.float32) * present[0].astype(jnp.float32)).astype(jnp.bfloat16)
    load_diag.wait()
    pl.semaphore_wait(barrier, NB - 1 + 2)

    def band_copy(half, dy, dz):
        first, second = (dz, dy) if half == 0 else (dy, dz)
        done, hop = (first, second) if second else (0, first)
        before = 0
        if second == 2:
            hop, before = (1, 1) if first < 2 else (-1, -1)
        if half == 0:
            source, there = at(-before, -done), (at(hop, 0) if second else at(0, hop))
        else:
            source, there = at(-done, -before), (at(0, hop) if second else at(hop, 0))
        i = half * (NB - 1) + dy * SIDE + dz - 1
        return remote(bands.at[half, source], bands.at[half, source], band_send.at[i], band_recv.at[i], col=there)

    def band_wait(half, dy, dz):
        i = half * (NB - 1) + dy * SIDE + dz - 1
        block = bands.at[half, at(-dy, -dz)]
        remote(block, block, band_send.at[i], band_recv.at[i], col=at(dy, dz)).wait_recv()

    def band_part(half, side):
        hop = 1 - 2 * side
        along = (lambda step: at(0, step)) if half == 0 else (lambda step: at(step, 0))
        part = bands.at[half, along(-hop), pl.ds(side * (W // 2), W // 2)]
        i = 2 * (NB - 1) + 2 * half + side
        return remote(part, part, band_send.at[i], band_recv.at[i], col=along(hop))

    def band_part_wait(half, side):
        along = (lambda step: at(0, step)) if half == 0 else (lambda step: at(step, 0))
        part = bands.at[half, along(2), pl.ds(side * (W // 2), W // 2)]
        i = 2 * (NB - 1) + 2 * half + side
        remote(part, part, band_send.at[i], band_recv.at[i], col=along(1)).wait_recv()

    for d in (1, SIDE - 1):
        band_copy(0, 0, d).start()
        band_copy(1, d, 0).start()
    halo_up = [remote(columns.at[pl.ds(rows_here - W, W)], v0.at[pl.ds(0, W)], halo_send.at[0], halo_recv.at[0], row=up)]
    halo_down = [remote(columns.at[pl.ds(0, W)], v0.at[pl.ds(rows_here + W, W)], halo_send.at[1], halo_recv.at[1], row=down)]
    for degree, v in ((1, v1), (2, v2)):
        halo_up.append(
            remote(v.at[pl.ds(rows_here, W)], v.at[pl.ds(0, W)], halo_send.at[2 * degree], halo_recv.at[2 * degree], row=up)
        )
        halo_down.append(
            remote(
                v.at[pl.ds(W, W)],
                v.at[pl.ds(rows_here + W, W)],
                halo_send.at[2 * degree + 1],
                halo_recv.at[2 * degree + 1],
                row=down,
            )
        )
    halo_up[0].start()
    halo_down[0].start()
    meta_copies = [
        remote(meta_out.at[k, pl.ds(0, 1)], meta_in.at[k, pl.ds(0, 1)], meta_send.at[k], meta_recv.at[k], col=at(*OFF[k]))
        for k in range(1, NB)
    ]
    meta_copies += [
        remote(core_out.at[pl.ds(0, SLOTS)], core_in.at[k, pl.ds(0, SLOTS)], core_send.at[k], core_recv.at[k], col=at(*OFF[k]))
        for k in range(1, NB)
    ]
    for copy in meta_copies:
        copy.start()

    part = 2 * KB // PIECES
    pieces = [(s, half, first) for s in range(CAP) for half in range(2) for first in range(0, KB, part)]

    def send_pieces(s, half, first):
        for k in range(1, NB):
            i = s * NB + k
            remote(
                outgoing.at[i, half, pl.ds(first, part)],
                incoming.at[i, half, pl.ds(first, part)],
                basis_send.at[i],
                basis_recv.at[i],
                col=at(*OFF[k]),
            ).start()

    load_basis.wait()
    for s in range(CAP):
        incoming[s * NB] = basis_vm[owner[s * NB]]

        def pack(k, carry, s=s):
            outgoing[s * NB + k] = basis_vm[owner[s * NB + k]]
            return carry

        lax.fori_loop(1, NB, pack, 0)
        if s == 0:
            for piece in pieces[:EARLY]:
                send_pieces(*piece)

    for side, d in ((0, 1), (1, SIDE - 1)):
        for half, (dy, dz) in enumerate(((0, d), (d, 0))):
            band_wait(half, dy, dz)
            band_part(half, side).start()
    for d in (0, 1, SIDE - 1, 2):
        if d == 2:
            for half in range(2):
                band_part_wait(half, 0)
                band_part_wait(half, 1)
        for other in (1, SIDE - 1):
            band_copy(0, other, d).start()
            band_copy(1, d, other).start()
    for piece in pieces[EARLY : EARLY + 1]:
        send_pieces(*piece)
    for d in range(SIDE):
        near = 1 if d < 2 else SIDE - 1
        band_wait(0, near, d)
        band_copy(0, 2, d).start()
        band_wait(1, d, near)
        band_copy(1, d, 2).start()
    for piece in pieces[EARLY + 1 :]:
        send_pieces(*piece)

    for first in range(SIDE):
        for second in (2, SIDE - 1 if first < 2 else 1):
            band_wait(0, second, first)
            band_wait(1, first, second)

    row_at = lax.broadcasted_iota(jnp.int32, (W, W), 0)
    col_at = lax.broadcasted_iota(jnp.int32, (W, W), 1)

    def build(j, carry):
        coupling = bands[1, j].astype(jnp.float32)
        first = jnp.where((j == 0) & (r == 0), 0.0, 1.0)
        last = jnp.where((j == NB - 1) & (r == rows - 1), 0.0, 1.0)
        band[j, :, 0:W] = (jnp.where(col_at >= row_at, coupling, 0.0) * first).astype(jnp.bfloat16)
        band[j, :, W : 2 * W] = bands[0, j]
        band[j, :, 2 * W : 3 * W] = (jnp.where(col_at < row_at, coupling, 0.0) * last).astype(jnp.bfloat16)
        return carry

    lax.fori_loop(0, NB, build, 0)

    def apply(j, v):
        window = v[pl.ds(pl.multiple_of(j * W, W), 3 * W), :]
        return jnp.dot(band[j], window, preferred_element_type=jnp.float32)

    def inner(j):
        return pl.ds(pl.multiple_of((j + 1) * W, W), W)

    def degree_1(j, carry):
        value = apply(j, v0)
        total[j] = value
        v1[inner(j), :] = value.astype(jnp.bfloat16)
        return carry

    c0, c1, c2, c3 = (coef[i] for i in range(4))

    def degree_2(j, carry):
        start = v0[inner(j), :].astype(jnp.float32)
        value = 2.0 * apply(j, v1) - start
        v2[inner(j), :] = value.astype(jnp.bfloat16)
        total[j] = c0 * start + (c1 - c3) * total[j] + c2 * value
        return carry

    def degree_3(j, carry):
        value = total[j] + (2.0 * c3) * apply(j, v2)
        kern[j // 2, pl.ds(pl.multiple_of(lax.rem(j, 2) * W, W), W), :] = value.astype(jnp.bfloat16)
        return carry

    load_columns.wait()
    halo_up[0].wait()
    halo_down[0].wait()
    for step, degree in ((degree_1, 1), (degree_2, 2)):
        step(0, 0)
        step(NB - 1, 0)
        lax.fori_loop(1, NB // 2, step, 0)
        halo_up[degree].start()
        halo_down[degree].start()
        lax.fori_loop(NB // 2, NB - 1, step, 0)
        halo_up[degree].wait()
        halo_down[degree].wait()
    lax.fori_loop(0, NB, degree_3, 0)

    for half, skip in enumerate(((0, 2), (2, 0))):
        for dy, dz in OFFSETS:
            if (dy, dz) != skip:
                band_copy(half, dy, dz).wait_send()
        for side in range(2):
            band_part(half, side).wait_send()
    for copy in meta_copies:
        copy.wait()
    meta_copy = pltpu.make_async_copy(meta_in.at[:, pl.ds(0, 1)], meta_sm.at[:, pl.ds(0, 1)], local_sem.at[4])
    meta_copy.start()
    meta_copy.wait()
    for s in range(CAP):
        for k in range(NB):
            block_of[s * NB + k] = meta_sm[k, 0, ENTRIES + s]

    def basis_copy(i):
        return remote(outgoing.at[i], incoming.at[i], basis_send.at[i], basis_recv.at[i], col=at(0, 1))

    def project(s, k):
        i = s * NB + k
        keep = pltpu.make_async_copy(incoming.at[i], received.at[i], out_sem.at[i])
        keep.start()
        block = jnp.maximum(meta_sm[k, 0, ENTRIES + s], 0)
        product = jnp.dot(kern[block], incoming[i, 1], preferred_element_type=jnp.float32)
        return jnp.sum(product * incoming[i, 0].astype(jnp.float32), axis=0, keepdims=True) * (1.0 / KB)

    contrib_copies = []
    groups = ((0, 0, NB), (1, 0, NB // 2), (1, NB // 2, NB))
    for g, (s, begin, end) in enumerate(groups):
        if begin == 0:
            contrib[c, s * NB : s * NB + 1, :] = project(s, 0)

        def step(k, carry, s=s):
            basis_copy(s * NB + k).wait_recv()
            contrib[c, pl.ds(s * NB + k, 1), :] = project(s, k)
            return carry

        lax.fori_loop(max(begin, 1), end, step, 0)
        rows_of = pl.ds(s * NB + begin, end - begin)
        lines = contrib.at[c, rows_of]
        for k in range(1, NB):
            i = g * NB + k
            copy = remote(lines, lines, contrib_send.at[i], contrib_recv.at[i], col=at(*OFF[k]))
            copy.start()
            contrib_copies.append(copy)
    def finish(k, carry):
        for s in range(CAP):
            basis_copy(s * NB + k).wait_send()
        return carry

    lax.fori_loop(1, NB, finish, 0)

    def kept(i, carry):
        pltpu.make_async_copy(incoming.at[i], received.at[i], out_sem.at[i]).wait()
        return carry

    lax.fori_loop(0, CAP * NB, kept, 0)

    for g, (s, begin, end) in enumerate(groups):
        for k in range(1, NB):
            i = g * NB + k
            lines = contrib.at[at(-OFF[k][0], -OFF[k][1]), pl.ds(s * NB + begin, end - begin)]
            remote(lines, lines, contrib_send.at[i], contrib_recv.at[i], col=at(0, 1)).wait_recv()

    for copy in contrib_copies:
        copy.wait_send()

    def density_of(k, tile):
        value = core_in[k, pl.ds(tile, 1), :]
        for slot in range(SLOTS):
            place = meta_sm[k, 0, tile * SLOTS + slot]
            there = jnp.maximum(place, 0)
            line = contrib[lax.div(there, CAP * NB), pl.ds(lax.rem(there, CAP * NB), 1), :]
            value = value + jnp.where(place >= 0, line, 0.0)
        return value

    for t in range(ENTRIES // SLOTS):
        dens[t : t + 1, :] = density_of(0, t)

    def slot_density(k, carry):
        for s in range(CAP):
            tile_density[pl.ds(s * NB + k, 1), :] = density_of(k, meta_sm[k, 0, ENTRIES + CAP + s])
        return carry

    lax.fori_loop(0, NB, slot_density, 0, unroll=True)
    x = jnp.maximum(tile_density[...], 0.1)
    root = jnp.exp(jnp.log(x) * (1.0 / 3.0))
    root = root - (root * root * root - x) / (3.0 * root * root)
    pot_in[...] = -exchange_factor * root


def exchange(columns, ham, pattern, coef, peers, tile_block, tile_count, basis, core):
    any_spec = pl.BlockSpec(memory_space=pl.ANY)
    smem = pl.BlockSpec(memory_space=pltpu.SMEM)
    vmem = pl.BlockSpec(memory_space=pltpu.VMEM)
    rows_here = NB * W
    slots = CAP * NB
    bf16, f32, i32 = jnp.bfloat16, jnp.float32, jnp.int32
    dma = pltpu.SemaphoreType.DMA
    return pl.pallas_call(
        exchange_kernel,
        out_shape=(
            jax.ShapeDtypeStruct(core.shape, f32),
            jax.ShapeDtypeStruct((slots, 2, KB, P_SIZE), bf16),
            jax.ShapeDtypeStruct((slots, P_SIZE), f32),
            jax.ShapeDtypeStruct((slots,), i32),
        ),
        in_specs=[any_spec] * 9,
        out_specs=(vmem, any_spec, vmem, smem),
        scratch_shapes=[
            pltpu.SMEM((1,), i32),
            pltpu.SMEM(coef.shape, f32),
            pltpu.SMEM(peers.shape, i32),
            pltpu.SMEM(tile_block.shape, i32),
            pltpu.SMEM(tile_count.shape, i32),
            pltpu.VMEM(core.shape, f32),
            pltpu.VMEM((W, W), bf16),
            pltpu.VMEM((2, NB, W, W), bf16),
            pltpu.VMEM((NB, W, 3 * W), bf16),
            pltpu.VMEM((rows_here + 2 * W, KB), bf16),
            pltpu.VMEM((rows_here + 2 * W, KB), bf16),
            pltpu.VMEM((rows_here + 2 * W, KB), bf16),
            pltpu.VMEM((NB, W, KB), f32),
            pltpu.VMEM((rows_here // KB, KB, KB), bf16),
            pltpu.VMEM(basis.shape, bf16),
            pltpu.VMEM((slots, 2, KB, P_SIZE), bf16),
            pltpu.VMEM((slots, 2, KB, P_SIZE), bf16),
            pltpu.VMEM((NB, 8, P_SIZE), i32),
            pltpu.VMEM((NB, 8, P_SIZE), i32),
            pltpu.SMEM((NB, 8, P_SIZE), i32),
            pltpu.VMEM((8, P_SIZE), f32),
            pltpu.VMEM((NB, 8, P_SIZE), f32),
            pltpu.VMEM((NB, slots, P_SIZE), f32),
            pltpu.VMEM((slots, P_SIZE), f32),
            pltpu.SMEM((slots,), i32),
            dma((11,)),
            dma((slots,)),
            dma((2 * (NB - 1) + 4,)),
            dma((2 * (NB - 1) + 4,)),
            dma((NB,)),
            dma((NB,)),
            dma((6,)),
            dma((6,)),
            dma((slots,)),
            dma((slots,)),
            dma((3 * NB,)),
            dma((3 * NB,)),
            dma((NB,)),
            dma((NB,)),
        ],
        compiler_params=pltpu.CompilerParams(
            collective_id=0, has_side_effects=True, vmem_limit_bytes=66_000_000
        ),
        name="exchange",
    )(columns, ham, pattern, coef, peers, tile_block, tile_count, basis, core)


def update_kernel(
    received, pot, block_of, density, out, dens, pairs, lines, blocks, named, count, total, rounded, points, pair_sem, sem
):
    slots = CAP * NB
    row_blocks = NB * W // KB
    load_blocks = pltpu.make_async_copy(block_of, blocks, sem.at[0])
    load_lines = pltpu.make_async_copy(pot, lines, sem.at[1])
    load_blocks.start()
    load_lines.start()
    load_points = pltpu.make_async_copy(density, points, sem.at[2 + row_blocks])
    store_points = pltpu.make_async_copy(points, dens, sem.at[3 + row_blocks])
    load_points.start()
    for b in range(row_blocks):
        count[b] = 0
    load_blocks.wait()

    def load(i):
        return pltpu.make_async_copy(received.at[i], pairs.at[i], pair_sem.at[i])

    def sort(i, carry):
        block = blocks[i]

        @pl.when(block >= 0)
        def _():
            named[block * slots + count[block]] = i
            count[block] = count[block] + 1

        return carry

    lax.fori_loop(0, slots, sort, 0)

    def fetch(b, carry):
        def one(j, carry):
            load(named[b * slots + j]).start()
            return carry

        return lax.fori_loop(0, count[b], one, carry)

    lax.fori_loop(0, row_blocks, fetch, 0)
    load_lines.wait()
    load_points.wait()
    store_points.start()

    def store(b):
        return pltpu.make_async_copy(rounded.at[b], out.at[b], sem.at[2 + b])

    def weighted(i, present):
        line = jnp.where(present, lines[pl.ds(i, 1), :], 0.0)
        return (pairs[i, 1].astype(jnp.float32) * line).astype(jnp.bfloat16)

    def product(b, j, n, group):
        first = named[b * slots + group * j]
        left, right = [], []
        for q in range(group):
            here = group * j + q < n
            i = jnp.where(here, named[b * slots + group * j + q], first)

            @pl.when(here)
            def _(i=i):
                load(i).wait()

            left.append(i)
            right.append(here)
        return lax.dot_general(
            jnp.concatenate([pairs[i, 0] for i in left], axis=1),
            jnp.concatenate([weighted(i, here) for i, here in zip(left, right)], axis=1),
            (((1,), (1,)), ((), ())),
            preferred_element_type=jnp.float32,
        )

    scale = 1.0 / math.sqrt(P_SIZE)

    def block_sum(b, carry):
        n = count[b]

        for fewer, group in ((0, 2), (2, GROUP)):

            @pl.when((n > fewer) & (n <= group))
            def _(group=group):
                rounded[b] = (product(b, 0, n, group) * scale).astype(jnp.bfloat16)

        @pl.when(n > GROUP)
        def _():
            total[...] = jnp.zeros_like(total)

            def add(j, carry):
                total[...] = total[...] + product(b, j, n, GROUP)
                return carry

            lax.fori_loop(0, lax.div(n + GROUP - 1, GROUP), add, 0)
            rounded[b] = (total[...] * scale).astype(jnp.bfloat16)

        @pl.when(n > 0)
        def _():
            store(b).start()

        return carry

    def clear(b, carry):
        @pl.when(count[b] == 0)
        def _():
            rounded[b] = jnp.zeros((KB, KB), jnp.bfloat16)
            store(b).start()

        return carry

    lax.fori_loop(0, row_blocks, clear, 0)
    lax.fori_loop(0, row_blocks, block_sum, 0)
    for b in range(row_blocks):
        store(b).wait()
    store_points.wait()


def update(block_of, received, pot_in, density):
    blocks = NB * W // KB
    any_spec = pl.BlockSpec(memory_space=pl.ANY)
    return pl.pallas_call(
        update_kernel,
        out_shape=(
            jax.ShapeDtypeStruct((blocks, KB, KB), jnp.bfloat16),
            jax.ShapeDtypeStruct(density.shape, density.dtype),
        ),
        in_specs=[any_spec] * 4,
        out_specs=(any_spec, any_spec),
        scratch_shapes=[
            pltpu.VMEM(received.shape, received.dtype),
            pltpu.VMEM(pot_in.shape, pot_in.dtype),
            pltpu.SMEM(block_of.shape, block_of.dtype),
            pltpu.SMEM((blocks * CAP * NB,), jnp.int32),
            pltpu.SMEM((blocks,), jnp.int32),
            pltpu.VMEM((KB, KB), jnp.float32),
            pltpu.VMEM((blocks, KB, KB), jnp.bfloat16),
            pltpu.VMEM(density.shape, density.dtype),
            pltpu.SemaphoreType.DMA((CAP * NB,)),
            pltpu.SemaphoreType.DMA((4 + blocks,)),
        ],
        compiler_params=pltpu.CompilerParams(vmem_limit_bytes=67_000_000),
        name="update",
    )(received, pot_in, block_of, density)


def shards(columns, ham, pattern, coef, peers, tile_block, tile_count, basis, core):
    dens, received, pot_in, block_of = exchange(
        columns, ham, pattern, coef, peers.reshape(-1), tile_block, tile_count, basis, core
    )
    blocks, dens = update(block_of, received, pot_in, dens)
    return dens, blocks.reshape(columns.shape)


def solution(mesh):
    return jax.shard_map(
        shards,
        mesh=mesh,
        in_specs=(
            P("row", "col"),
            P(("row", "col"), None, None, None),
            P(("row", "col")),
            P(),
            P(("row", "col"), None),
            P(("row", "col")),
            P(("row", "col")),
            P(("row", "col"), None, None, None),
            P(("row", "col"), None),
        ),
        out_specs=(P(("row", "col"), None), P("row", "col")),
        check_vma=False,
    )
```
